128 devices in a mesh: seq: 16 (over x, z), ch: 8 (over y, core).
Axes of the slice: x: 4, y: 4, z: 4, core: 2. Of those that a mesh axis runs over, the one named last changes fastest.
Arguments:
- features: bfloat16 [2048, 8192], P('seq', 'ch'), may hold values from -6 to 6
- qkv_weight: bfloat16 [1664, 3, 8192], P('seq', None, 'ch'), may hold values from -0.0625 to 0.0625
- grad_out: bfloat16 [1664, 2048], P('ch', 'seq'), may hold values from -6 to 6
- residues: float32 [1664, 16], P('ch'), may hold values from -1 to 1
- log_rates: float32 [1664, 16], P('ch'), may hold values from -10 to -1, as said below
- skip_gain: float32 [1664], P('ch'), may hold values from -1 to 1
Outputs:
- weight_grad: float32 [1664, 3, 8192], P('seq', None, 'ch')
- residue_grad: float32 [1664, 16], P('ch')
- rate_grad: float32 [1664, 16], P('ch')
- skip_grad: float32 [1664], P('ch')
The draws below stay inside these ranges and needn't reach their ends.
Inputs may be any that keep to these rules, and one draw needn't show every extreme that they name: Each channel's decay rates exp(log_rates) lie between about 1 / 2048 and 3 / 20.
All inputs are finite; a program needn't handle non-finite values.
Results may differ from the reference program's by a relative error of at most 0.029.
Values may be sent and summed in bfloat16 or wider, within the bound.
A program may use at most 64 MiB of HBM per device.

```python
import math
import jax
import jax.numpy as jnp
from jax import lax

D = 8192
C = 1664
ORDER = 16
TOK_DEV = 128
TOKENS = 2048
N_SEQ = 16


def decay_logs(key):
    fraction = jax.random.uniform(jax.random.fold_in(key, 11), (C, 1), jnp.float32)
    fraction = 1.0 - (1.0 - fraction) ** 3
    fastest = math.log(1.0 / 20.0)
    slowest = math.log(1.0 / TOKENS)
    baseline = fastest + fraction * (slowest - fastest)
    spread = jax.random.uniform(jax.random.fold_in(key, 12), (C, ORDER), jnp.float32, 0.0, math.log(3.0))
    return baseline + spread


def draw_log_rates(key, part):
    return decay_logs(key)


def draw_residues(key, part):
    rates = jnp.exp(decay_logs(key))
    normals = jnp.clip(jax.random.normal(jax.random.fold_in(key, 13), (C, ORDER), jnp.float32), -4.0, 4.0)
    return normals * jnp.sqrt(2.0 * rates / ORDER)


def steps_of(stream_key, shape, cuts, smallest, largest):
    level = 1.0
    for dim, parts in cuts:
        heights = jax.random.uniform(jax.random.fold_in(jax.random.fold_in(stream_key, 6), dim), (parts,), jnp.float32, smallest / len(cuts), largest / len(cuts))
        level = level * jnp.repeat(jnp.exp(heights), shape[dim] // parts).reshape((-1,) + (1,) * (len(shape) - 1 - dim))
    return level


def gaussian(stream_key, shape, scale, reach, split=(), kind=jnp.bfloat16):
    factor_of = steps_of(stream_key, shape, split, -0.22, 0.18) if split else 1.0
    entries = jax.random.normal(stream_key, shape, jnp.float32) * scale * factor_of
    return jnp.minimum(jnp.maximum(entries, -reach), reach).astype(kind)


def setup_inputs(seed: int = 0) -> dict:
    seeds = jax.random.split(jax.random.key(seed), 7)
    features = gaussian(seeds[0], (TOKENS, D), 1.0, 6.0, ((0, 16), (1, 8)))
    qkv_weight = gaussian(seeds[1], (C, 3, D), D ** -0.5, 0.0625, ((0, 16), (2, 8)))
    grad_out = gaussian(seeds[2], (C, TOKENS), 1.0, 6.0, ((0, 8), (1, 16)))
    residues = draw_residues(jax.random.fold_in(seeds[6], 71), 0)
    log_rates = draw_log_rates(jax.random.fold_in(seeds[6], 71), 0)
    skip_gain = jnp.clip(jax.random.uniform(seeds[5], (C,), jnp.float32, -1.0, 1.0) * steps_of(seeds[5], (C,), ((0, 8),), -0.4, 0.0), -1.0, 1.0)
    return {"features": features, "qkv_weight": qkv_weight, "grad_out": grad_out, "residues": residues, "log_rates": log_rates, "skip_gain": skip_gain}


def reference(features, qkv_weight, grad_out, residues, log_rates, skip_gain):
    period = 2 * TOKENS
    flat_weight = qkv_weight.reshape(C * 3, D)
    projected = jnp.dot(features, flat_weight.T, preferred_element_type=jnp.float32).astype(jnp.bfloat16)
    projected = projected.reshape(TOKENS, C, 3).transpose(1, 2, 0)
    queries = projected[:, 0].astype(jnp.float32)
    keys = projected[:, 1].astype(jnp.float32)
    values = projected[:, 2].astype(jnp.float32)
    kv_product = keys * values
    rates = jnp.exp(log_rates)
    steps = jnp.arange(TOKENS, dtype=jnp.float32)
    taps = jnp.zeros((C, TOKENS), jnp.float32)
    for order_index in range(ORDER):
        taps = taps + residues[:, order_index:order_index + 1] * jnp.exp(-rates[:, order_index:order_index + 1] * steps[None, :])
    spec_mixed = jnp.fft.rfft(kv_product, n=period, axis=1)
    spec_taps = jnp.fft.rfft(taps, n=period, axis=1)
    conv_out = jnp.fft.irfft(spec_taps * spec_mixed, n=period, axis=1)[:, :TOKENS]
    grad_upper = grad_out.astype(jnp.float32)
    grad_mid = grad_upper * queries
    spec_mid = jnp.fft.rfft(grad_mid, n=period, axis=1)
    corr_out = jnp.fft.irfft(jnp.conj(spec_taps) * spec_mid, n=period, axis=1)[:, :TOKENS]
    taps_grad = jnp.fft.irfft(jnp.conj(spec_mixed) * spec_mid, n=period, axis=1)[:, :TOKENS]
    skip_col = skip_gain[:, None]
    grad_query = grad_upper * (conv_out + skip_col * kv_product)
    grad_mix = corr_out + skip_col * grad_mid
    grad_proj = jnp.stack([grad_query, grad_mix * values, grad_mix * keys], axis=1).astype(jnp.bfloat16)
    grad_blocks = grad_proj.reshape(C * 3, N_SEQ, TOK_DEV).transpose(1, 0, 2)
    feature_blocks = features.reshape(N_SEQ, TOK_DEV, D)

    def add_block(total, pieces):
        grad_piece, feature_piece = pieces
        partial_sum = jnp.dot(grad_piece, feature_piece, preferred_element_type=jnp.float32)
        rounded = lax.optimization_barrier(partial_sum.astype(jnp.bfloat16))
        return total + rounded.astype(jnp.float32), None

    weight_total, _ = lax.scan(add_block, jnp.zeros((C * 3, D), jnp.float32), (grad_blocks, feature_blocks))
    weight_grad = weight_total.reshape(C, 3, D)
    residue_cols = []
    rate_cols = []
    for order_index in range(ORDER):
        decays = jnp.exp(-rates[:, order_index:order_index + 1] * steps[None, :])
        residue_cols.append(jnp.sum(taps_grad * decays, axis=1))
        moment = jnp.sum(taps_grad * steps[None, :] * decays, axis=1)
        rate_cols.append(-residues[:, order_index] * rates[:, order_index] * moment)
    residue_grad = jnp.stack(residue_cols, axis=1)
    rate_grad = jnp.stack(rate_cols, axis=1)
    skip_grad = jnp.sum(grad_mid * kv_product, axis=1)
    return weight_grad, residue_grad, rate_grad, skip_grad
```

```python
import jax
import jax.numpy as jnp
from jax import lax
from jax.sharding import PartitionSpec as P

CHUNK = 128


def decays_of(rates, lags):
    return jnp.exp(-rates[:, :, None] * lags[None, None, :])


def toeplitz(taps):
    rows = jnp.arange(CHUNK)
    lag = rows[None, :] - rows[:, None]
    picked = jnp.take(taps, jnp.maximum(lag, 0).reshape(-1), axis=1).reshape(-1, CHUNK, CHUNK)
    return jnp.where(lag[None] >= 0, picked, 0.0)


def diagonal_sums(product):
    padded = jnp.pad(product, ((0, 0), (0, 0), (0, CHUNK)))
    flat = padded.reshape(product.shape[0], -1)[:, : CHUNK * (2 * CHUNK - 1)]
    skewed = flat.reshape(-1, CHUNK, 2 * CHUNK - 1)
    return skewed.sum(axis=1)


def mix(projected, grads, residues, log_rates, gain):
    count = projected.shape[0]
    chunks = projected.shape[2] // CHUNK
    parts = projected.astype(jnp.float32).reshape(count, 3, chunks, CHUNK)
    queries, keys, values = parts[:, 0], parts[:, 1], parts[:, 2]
    grad_upper = grads.astype(jnp.float32).reshape(count, chunks, CHUNK)
    kv = keys * values
    gm = grad_upper * queries
    rates = jnp.exp(log_rates)
    lags = jnp.arange(CHUNK, dtype=jnp.float32)
    near = decays_of(rates, lags)
    far = decays_of(rates, CHUNK - lags)
    taps = (residues[:, :, None] * near).sum(axis=1)
    band = toeplitz(taps)
    conv = jnp.einsum("ckb,cba->cka", kv, band)
    corr = jnp.einsum("cka,cba->ckb", gm, band)
    tails = jnp.einsum("ckb,crb->kcr", kv, far)
    tails_lag = jnp.einsum("ckb,crb->kcr", kv, far * (CHUNK - lags))
    heads = jnp.einsum("cka,cra->kcr", gm, near)
    heads_lag = jnp.einsum("cka,cra->kcr", gm, near * lags)
    step = jnp.exp(-CHUNK * rates)
    state = jnp.zeros_like(step)
    state_lag = jnp.zeros_like(step)
    states, states_lag = [], []
    for k in range(chunks):
        states.append(state)
        states_lag.append(state_lag)
        state_lag = step * (state_lag + CHUNK * state) + tails_lag[k]
        state = step * state + tails[k]
    adjoint = jnp.zeros_like(step)
    adjoints = []
    for k in reversed(range(chunks)):
        adjoints.append(adjoint)
        adjoint = step * adjoint + heads[k]
    states = jnp.stack(states)
    states_lag = jnp.stack(states_lag)
    adjoints = jnp.stack(adjoints[::-1])
    conv = conv + jnp.einsum("kcr,cra->cka", states * residues, near)
    corr = corr + jnp.einsum("kcr,crb->ckb", adjoints * residues, far)
    product = jnp.einsum("cka,ckb->cba", gm, kv)
    rolled = jnp.where((lags[None, :] >= lags[:, None])[None], product, 0.0)
    sums = diagonal_sums(rolled[:, ::-1])[:, CHUNK - 1 :]
    residue_grad = jnp.einsum("cj,crj->cr", sums, near, precision="highest") + (heads * states).sum(0)
    moment = jnp.einsum("cj,crj->cr", sums * lags, near, precision="highest") + (
        heads_lag * states + heads * states_lag
    ).sum(0)
    rate_grad = -residues * rates * moment
    skip_grad = (gm * kv).sum((1, 2))
    col = gain[:, None, None]
    grad_query = grad_upper * (conv + col * kv)
    grad_mix = corr + col * gm
    grad_proj = jnp.stack([grad_query, grad_mix * values, grad_mix * keys], axis=1)
    grad_proj = grad_proj.astype(jnp.bfloat16).reshape(count, 3, -1)
    return grad_proj, residue_grad, rate_grad, skip_grad


def local(features, qkv_weight, grad_out, residues, log_rates, skip_gain):
    seq = lax.axis_index("seq")
    ch = lax.axis_index("ch")
    ways = lax.axis_size("ch")
    every = lax.all_gather(features, "seq", axis=0, tiled=True)
    per = qkv_weight.shape[0] // ways

    def to_owner(rows):
        halves = rows.reshape(2, ways, per, *rows.shape[1:])
        picked = lax.dynamic_index_in_dim(halves, seq % 2, 0, keepdims=False)
        arrived = lax.all_to_all(picked, "ch", split_axis=0, concat_axis=0, tiled=True)
        return lax.dynamic_index_in_dim(arrived, seq // 2, 0, keepdims=False)

    grads = to_owner(lax.all_gather(grad_out, "seq", axis=1, tiled=True))
    packed = to_owner(jnp.concatenate([residues, log_rates, skip_gain[:, None]], axis=1))
    order = residues.shape[1]
    partial = jnp.einsum("cgd,td->cgt", qkv_weight, every, preferred_element_type=jnp.float32)
    tiles = partial.astype(jnp.bfloat16).reshape(ways, per, *partial.shape[1:])
    arrived = lax.all_to_all(tiles, "ch", split_axis=0, concat_axis=0, tiled=True)
    projected = arrived.astype(jnp.float32).sum(axis=0).astype(jnp.bfloat16)
    grad_proj, residue_grad, rate_grad, skip_grad = mix(
        projected, grads, packed[:, :order], packed[:, order : 2 * order], packed[:, 2 * order]
    )
    full = lax.all_gather(grad_proj, "ch", axis=0, tiled=True)
    weight_grad = jnp.einsum("cgt,td->cgd", full, every, preferred_element_type=jnp.float32)
    small = jnp.concatenate([residue_grad, rate_grad, skip_grad[:, None]], axis=1)
    gathered = lax.all_gather(small, ("seq", "ch"), axis=0, tiled=True)
    block = residues.shape[0]
    own = lax.dynamic_slice_in_dim(gathered, ch * block, block, 0)
    return weight_grad, own[:, :order], own[:, order : 2 * order], own[:, 2 * order]


def solution(mesh):
    placed = (
        P("seq", "ch"),
        P("seq", None, "ch"),
        P("ch", "seq"),
        P("ch", None),
        P("ch", None),
        P("ch"),
    )
    return jax.shard_map(
        local,
        mesh=mesh,
        in_specs=placed,
        out_specs=(P("seq", None, "ch"), P("ch", None), P("ch", None), P("ch")),
        check_vma=False,
    )
```

```python
import functools

import jax
import jax.numpy as jnp
from jax import lax
from jax.experimental import pallas as pl
from jax.experimental.pallas import tpu as pltpu
from jax.sharding import PartitionSpec as P

F32, BF16 = jnp.float32, jnp.bfloat16
CHUNK = 128
SIDE = 4
SHARDS = SIDE * SIDE
WAYS = 2 * SIDE
ROWS = 16
TRIO = 3 * ROWS
STATE = 16
MESH = pl.DeviceIdType.MESH
PARAM_ROWS = 5 * ROWS

NT = (((1,), (1,)), ((), ()))
TN = (((0,), (0,)), ((), ()))
NN = (((1,), (0,)), ((), ()))


def mul(a, b, dims=NN):
    return lax.dot_general(a, b, dims, preferred_element_type=F32)


def iota(shape, dim):
    return lax.broadcasted_iota(jnp.int32, shape, dim)


def sum_partials(parts, grads, kvs, gms, grs, proj):
    flip = (iota((CHUNK, CHUNK), 0) + iota((CHUNK, CHUNK), 1) == CHUNK - 1).astype(BF16)

    def body(k, skip):
        total = parts[0, k].astype(F32)
        for way in range(1, WAYS):
            total = total + parts[way, k].astype(F32)
        rounded = total.astype(BF16)
        proj[k] = rounded
        wide = rounded.astype(F32)
        kv = wide[ROWS : 2 * ROWS] * wide[2 * ROWS :]
        gm = grads[k].astype(F32) * wide[:ROWS]
        kvs[k] = kv
        gms[k] = gm
        grs[k] = mul(gm.astype(BF16), flip)
        return skip + kv * gm

    return lax.fori_loop(0, SHARDS, body, jnp.zeros((ROWS, CHUNK), F32), unroll=4)


def carry(values, step, lagged, reverse):
    row = iota(values.shape, 0)
    shape = values.shape
    decay = jnp.broadcast_to(step, shape)
    reach = 1
    while reach < shape[0]:
        amount = shape[0] - reach if reverse else reach
        keep = row < shape[0] - reach if reverse else row >= reach
        near = jnp.where(keep, decay * pltpu.roll(values, amount, 0), 0.0)
        if lagged is not None:
            moved = jnp.where(keep, decay * pltpu.roll(lagged, amount, 0), 0.0)
            lagged = lagged + moved + (CHUNK * reach) * near
        values = values + near
        decay = decay * decay
        reach *= 2
    return values, lagged


def before(values, reverse):
    row = iota(values.shape, 0)
    last = values.shape[0] - 1
    if reverse:
        return jnp.where(row < last, pltpu.roll(values, last, 0), 0.0)
    return jnp.where(row >= 1, pltpu.roll(values, 1, 0), 0.0)


def mix_channel(c, params, kvs, gms, grs, convs, corrs, small):
    lane = iota((STATE, CHUNK), 1).astype(F32)
    rates = jnp.exp(params[0:STATE, c : c + 1])
    residues = params[STATE : 2 * STATE, c : c + 1]
    near = jnp.exp(-rates * lane)
    far = jnp.exp(-rates * (CHUNK - lane))
    taps = jnp.sum(residues * near, axis=0, keepdims=True)
    upper = iota((CHUNK, CHUNK), 1) >= iota((CHUNK, CHUNK), 0)
    spread = pltpu.roll(jnp.broadcast_to(taps, (CHUNK, CHUNK)), 0, 1, stride=1, stride_axis=0)
    band = jnp.where(upper, spread, 0.0).astype(BF16)
    kv = kvs[:, c, :].astype(BF16)
    gm = gms[:, c, :].astype(BF16)
    gr = grs[:, c, :].astype(BF16)
    near_b, far_b = near.astype(BF16), far.astype(BF16)
    near_lag = (near * lane).astype(BF16)
    far_lag = (far * (CHUNK - lane)).astype(BF16)
    tails = mul(kv, jnp.concatenate([far_b, far_b, far_b], 0), NT)
    tails_lag = mul(kv, jnp.concatenate([far_lag, far_lag, far_lag], 0), NT)
    heads = mul(gm, jnp.concatenate([near_b, near_lag, near_b], 0), NT)
    row_rates = jnp.exp(params[2 * STATE + c : 2 * STATE + c + 1, 0 : 3 * STATE])
    step = jnp.exp(-CHUNK * row_rates)
    row_residues = params[3 * STATE + c : 3 * STATE + c + 1, 0:STATE]
    states, states_lag = carry(tails, step, tails_lag, False)
    states, states_lag = before(states, False), before(states_lag, False)
    third = iota(states.shape, 1) < 2 * STATE
    inter = jnp.sum(heads * jnp.where(third, states, states_lag), axis=0, keepdims=True)
    adjoints, _ = carry(heads[:, 0:STATE], step[:, 0:STATE], None, True)
    adjoints = before(adjoints, True)
    conv = mul(kv, band) + mul((states[:, 0:STATE] * row_residues).astype(BF16), near_b)
    corr = mul(gm, band, NT) + mul((adjoints * row_residues).astype(BF16), far_b)
    convs[:, c, :] = conv
    corrs[:, c, :] = corr
    product = mul(kv, gr, TN)
    skewed = jnp.where(upper, pltpu.roll(product, 0, 1, stride=1, stride_axis=0), 0.0)
    sums = jnp.sum(skewed, axis=0, keepdims=True)
    back = far * jnp.exp(rates)
    weights = jnp.concatenate([back, back * (CHUNK - 1 - lane), jnp.zeros_like(back)], 0)
    wide = jnp.broadcast_to(sums, (ROWS, CHUNK)).astype(BF16)
    intra = mul(wide, weights.astype(BF16), NT)[0:1]
    small[c : c + 1, 0 : 3 * STATE] = inter + intra


def grads_of(params, grads, proj, kvs, gms, convs, corrs, mine):
    gain = params[4 * ROWS :, :]

    def body(k, _):
        wide = proj[k].astype(F32)
        keys, values = wide[ROWS : 2 * ROWS], wide[2 * ROWS :]
        grad_mix = corrs[k] + gain * gms[k]
        query = grads[k].astype(F32) * (convs[k] + gain * kvs[k])
        lanes = pl.ds(pl.multiple_of(k * CHUNK, CHUNK), CHUNK)
        mine[0:ROWS, lanes] = query.astype(BF16)
        mine[ROWS : 2 * ROWS, lanes] = (grad_mix * values).astype(BF16)
        mine[2 * ROWS :, lanes] = (grad_mix * keys).astype(BF16)
        return 0

    lax.fori_loop(0, SHARDS, body, 0, unroll=4)


def mix(count, params, parts, grads, kvs, gms, grs, proj, convs, corrs, small, mine):
    skip = sum_partials(parts, grads, kvs, gms, grs, proj)
    convs[...] = jnp.zeros_like(convs)
    corrs[...] = jnp.zeros_like(corrs)
    small[...] = jnp.zeros_like(small)
    for c in range(count):
        mix_channel(c, params, kvs, gms, grs, convs, corrs, small)
    lane = iota((ROWS, CHUNK), 1)
    summed = jnp.sum(skip, axis=1, keepdims=True)
    small[...] = jnp.where(lane == 3 * STATE, summed, small[...])
    grads_of(params, grads, proj, kvs, gms, convs, corrs, mine)


def kernel(
    count, feat, weight, gout, pars, wgrad, shared,
    every, wbuf, partial, parts, grads, params, kvs, gms, grs, proj, convs, corrs, small, full,
    local_sem, f_send, f_recv, r_send, r_recv, g_send, g_recv, p_send, p_recv, a_send, a_recv,
    s_send, s_recv,
):
    seq, ch = lax.axis_index("seq"), lax.axis_index("ch")
    x, z = seq // SIDE, seq % SIDE
    y, core = ch // 2, ch % 2
    home = seq // 2
    at_home = ch == home

    feat_in = pltpu.make_async_copy(feat, every.at[seq], local_sem.at[0])
    weight_in = pltpu.make_async_copy(weight, wbuf, local_sem.at[1])
    feat_in.start()
    weight_in.start()

    def ring(value, step):
        return (value + step + SIDE) % SIDE

    def place(v, p, q):
        return p * SIDE + q if v == 0 else q * SIDE + p

    def spot(v):
        return (x, z) if v == 0 else (z, x)

    barrier = pltpu.get_barrier_semaphore()

    def greet(s, c):
        pl.semaphore_signal(barrier, inc=1, device_id={"seq": s, "ch": c}, device_id_type=MESH)

    for v in range(2):
        p, q = spot(v)
        for step in (-1, 1):
            greet(place(v, ring(p, step), q), ch)
    for i in range(1, WAYS):
        greet(seq, (ch + i) % WAYS)

    def greet_far(i, _):
        @pl.when(jnp.logical_not(jnp.logical_and(i == seq, at_home)))
        def _():
            greet(i, home)

        @pl.when(jnp.logical_not(jnp.logical_and(2 * ch + i // WAYS == seq, i % WAYS == ch)))
        def _():
            greet(2 * ch + i // WAYS, i % WAYS)

        return 0

    lax.fori_loop(0, SHARDS, greet_far, 0)

    @pl.when(at_home)
    def _():
        pl.semaphore_wait(barrier, 4 + (WAYS - 1) + 2 * (SHARDS - 1))

    @pl.when(jnp.logical_not(at_home))
    def _():
        pl.semaphore_wait(barrier, 4 + (WAYS - 1) + 2 * SHARDS)

    half, quarter = CHUNK // 2, CHUNK // 4
    offs = (0, -1, 1, 2)

    def piece(v, part):
        start = v * half + (quarter if part == "b" else 0)
        return pl.ds(start, half if part == "h" else quarter)

    names = [("P1+", "h"), ("P1-", "h"), ("P2+", "a"), ("P2-", "b")]
    for j in range(3):
        names += [(f"Q1+{j}", "h"), (f"Q1-{j}", "h"), (f"Q2+{j}", "a"), (f"Q2-{j}", "b")]
    names += [("Q1+3a", "a"), ("Q1+3b", "b"), ("Q1-3a", "a"), ("Q1-3b", "b")]
    names += [("Q2+3", "a"), ("Q2-3", "b")]
    number = {name: n for n, (name, _) in enumerate(names)}
    piece_of = dict(names)

    def feature_copy(v, name, arriving):
        p, q = spot(v)
        step = 1 if name[2] == "+" else -1
        hops = int(name[1]) - 1 + (1 if arriving else 0)
        if name[0] == "P":
            source = place(v, ring(p, -step * hops), q)
            target = place(v, ring(p, step), q)
        else:
            source = place(v, ring(p, offs[int(name[3])]), ring(q, -step * hops))
            target = place(v, p, ring(q, step))
        rows = piece(v, piece_of[name])
        return pltpu.make_async_remote_copy(
            src_ref=every.at[source, rows],
            dst_ref=every.at[source, rows],
            send_sem=f_send.at[v, number[name]],
            recv_sem=f_recv.at[v, number[name]],
            device_id={"seq": target},
            device_id_type=MESH,
        )

    def send(v, name):
        feature_copy(v, name, False).start()

    def arrive(v, name):
        feature_copy(v, name, True).wait_recv()

    def owner_copy(shard, i):
        target = (ch + i) % WAYS
        return pltpu.make_async_remote_copy(
            src_ref=partial.at[shard, target],
            dst_ref=parts.at[i, shard],
            send_sem=r_send.at[i],
            recv_sem=r_recv.at[i],
            device_id={"ch": target},
            device_id_type=MESH,
        )

    def project(dx, dz):
        shard = ring(x, dx) * SIDE + ring(z, dz)
        out = mul(wbuf[...], every[shard], NT).astype(BF16).reshape(WAYS, TRIO, CHUNK)
        partial[shard] = out
        parts[0, shard] = partial[shard, ch]
        return shard

    def deliver(shard):
        for i in range(1, WAYS):
            owner_copy(shard, i).start()

    feat_in.wait()
    for v in range(2):
        send(v, "P1+")
        send(v, "P1-")
    for v in range(2):
        send(v, "Q1+0")
        send(v, "Q1-0")

    def grad_copy(i):
        return pltpu.make_async_remote_copy(
            src_ref=gout.at[i],
            dst_ref=grads.at[seq],
            send_sem=g_send.at[i],
            recv_sem=g_recv,
            device_id={"seq": 2 * ch + i // WAYS, "ch": i % WAYS},
            device_id_type=MESH,
        )

    def is_self(i):
        return jnp.logical_and(2 * ch + i // WAYS == seq, i % WAYS == ch)

    def start_grads(i, _):
        @pl.when(is_self(i))
        def _():
            pltpu.make_async_copy(gout.at[i], grads.at[seq], g_recv).start()

        @pl.when(jnp.logical_not(is_self(i)))
        def _():
            grad_copy(i).start()

        return 0

    lax.fori_loop(0, SHARDS, start_grads, 0)

    def param_copy(i):
        target = (ch + i) % WAYS
        return pltpu.make_async_remote_copy(
            src_ref=pars.at[target],
            dst_ref=params,
            send_sem=p_send.at[i],
            recv_sem=p_recv,
            device_id={"ch": target},
            device_id_type=MESH,
        )

    @pl.when(at_home)
    def _():
        pltpu.make_async_copy(pars.at[ch], params, p_recv).start()
        for i in range(1, WAYS):
            param_copy(i).start()

    weight_in.wait()
    done = [project(0, 0)]

    def follow(dx, dz):
        done.append(project(dx, dz))
        deliver(done[-2])

    for v in range(2):
        arrive(v, "P1+")
        send(v, "P2+")
        send(v, "Q1+1")
        send(v, "Q1-1")
        arrive(v, "P1-")
        send(v, "P2-")
        send(v, "Q1+2")
        send(v, "Q1-2")
    for v in range(2):
        arrive(v, "Q1+0")
        send(v, "Q2+0")
        arrive(v, "Q1-0")
        send(v, "Q2-0")
    for v in range(2):
        arrive(v, "P2+")
        send(v, "Q1+3a")
        send(v, "Q1-3a")
        arrive(v, "P2-")
        send(v, "Q1+3b")
        send(v, "Q1-3b")
    for dx, dz in ((-1, 0), (1, 0), (0, -1), (0, 1)):
        follow(dx, dz)
    for j in (1, 2):
        for v in range(2):
            arrive(v, f"Q1+{j}")
            send(v, f"Q2+{j}")
            arrive(v, f"Q1-{j}")
            send(v, f"Q2-{j}")
    for dx, dz in ((-1, -1), (-1, 1)):
        follow(dx, dz)
    for v in range(2):
        arrive(v, "Q1+3a")
        send(v, "Q2+3")
        arrive(v, "Q1-3b")
        send(v, "Q2-3")
    for dx, dz in ((1, -1), (1, 1)):
        follow(dx, dz)
    for v in range(2):
        arrive(v, "Q1+3b")
        arrive(v, "Q1-3a")
        arrive(v, "Q2+0")
        arrive(v, "Q2-0")
    for dx, dz in ((2, 0), (0, 2)):
        follow(dx, dz)
    for v in range(2):
        for j in (1, 2):
            arrive(v, f"Q2+{j}")
            arrive(v, f"Q2-{j}")
    for dx, dz in ((2, -1), (2, 1), (-1, 2), (1, 2)):
        follow(dx, dz)
    for v in range(2):
        arrive(v, "Q2+3")
        arrive(v, "Q2-3")
    follow(2, 2)
    deliver(done[-1])

    pltpu.make_async_copy(gout, grads, g_recv).wait()
    pltpu.make_async_copy(pars.at[0], params, p_recv).wait()
    for i in range(1, WAYS):
        pltpu.make_async_copy(parts.at[0], parts.at[i], r_recv.at[i]).wait()
    mix(count, params, parts, grads, kvs, gms, grs, proj, convs, corrs, small, full.at[0])

    width = SHARDS * CHUNK
    left, right = pl.ds(0, width // 2), pl.ds(width // 2, width // 2)

    def group_copy(n, source, target_slot, step, other, lanes=None):
        target = ring(y, step) * 2 + (1 - core if other else core)
        src, dst = full.at[source], full.at[target_slot]
        if lanes is not None:
            src, dst = full.at[source, :, lanes], full.at[target_slot, :, lanes]
        return pltpu.make_async_remote_copy(
            src_ref=src, dst_ref=dst, send_sem=a_send.at[n], recv_sem=a_recv.at[n],
            device_id={"ch": target}, device_id_type=MESH,
        )

    moves = [
        group_copy(0, 0, 6, 1, False),
        group_copy(1, 0, 2, -1, False),
        group_copy(2, 0, 1, 0, True),
        group_copy(3, 6, 4, 1, False, left),
        group_copy(4, 2, 4, -1, False, right),
        group_copy(5, 6, 7, 0, True),
        group_copy(6, 2, 3, 0, True),
        group_copy(7, 4, 5, 0, True, left),
        group_copy(8, 4, 5, 0, True, right),
    ]
    for n in (0, 1, 2):
        moves[n].start()

    def small_copy(i):
        return pltpu.make_async_remote_copy(
            src_ref=small,
            dst_ref=shared.at[(seq % 2) * WAYS + ch],
            send_sem=s_send.at[i],
            recv_sem=s_recv,
            device_id={"seq": i, "ch": home},
            device_id_type=MESH,
        )

    def small_self(i):
        return jnp.logical_and(i == seq, at_home)

    def start_small(i, _):
        @pl.when(small_self(i))
        def _():
            pltpu.make_async_copy(small, shared.at[(seq % 2) * WAYS + ch], s_recv).start()

        @pl.when(jnp.logical_not(small_self(i)))
        def _():
            small_copy(i).start()

        return 0

    lax.fori_loop(0, SHARDS, start_small, 0)

    tile = 256

    def weight_rows(slots, first, last):
        def body(n, _):
            lanes = pl.ds(pl.multiple_of(n * tile, tile), tile)
            left_side = jnp.concatenate([full[s] for s in slots], 0)
            right_side = every[:, :, lanes].reshape(width, tile)
            out = mul(left_side, right_side)
            for at, slot in enumerate(slots):
                owner = ring(y, slot // 2) * 2 + (1 - core if slot % 2 else core)
                rows = pl.ds(pl.multiple_of(owner * TRIO, TRIO), TRIO)
                wgrad[rows, lanes] = out[at * TRIO : (at + 1) * TRIO]
            return 0

        lax.fori_loop(first, last, body, 0)

    moves[0].wait_recv()
    moves[3].start()
    moves[5].start()
    moves[1].wait_recv()
    moves[4].start()
    moves[6].start()
    moves[2].wait_recv()
    weight_rows((0, 1, 2, 6), 0, 2)
    moves[3].wait_recv()
    moves[7].start()
    moves[4].wait_recv()
    moves[8].start()
    weight_rows((0, 1, 2, 6), 2, 4)
    for n in (5, 6, 7, 8):
        moves[n].wait_recv()
    weight_rows((3, 7, 4, 5), 0, 4)

    pltpu.make_async_copy(shared, shared, s_recv).wait()
    for move in moves:
        move.wait_send()
    for v in range(2):
        for name, _ in names:
            feature_copy(v, name, False).wait_send()
    for i in range(1, WAYS):
        pltpu.make_async_copy(parts.at[0], parts.at[i], r_send.at[i]).wait()

    def end_small(i, _):
        @pl.when(jnp.logical_not(is_self(i)))
        def _():
            grad_copy(i).wait_send()

        @pl.when(jnp.logical_not(small_self(i)))
        def _():
            small_copy(i).wait_send()

        return 0

    lax.fori_loop(0, SHARDS, end_small, 0)

    @pl.when(at_home)
    def _():
        for i in range(1, WAYS):
            param_copy(i).wait_send()


def local(features, qkv_weight, grad_out, residues, log_rates, skip_gain):
    seq = lax.axis_index("seq")
    width = features.shape[1]
    count = qkv_weight.shape[0] // WAYS
    spare = ROWS - count
    weight = qkv_weight.reshape(WAYS, count, 3, width).transpose(0, 2, 1, 3)
    weight = jnp.pad(weight, ((0, 0), (0, 0), (0, spare), (0, 0))).reshape(WAYS * TRIO, width)
    grads = jnp.pad(grad_out.reshape(2 * WAYS, count, CHUNK), ((0, 0), (0, spare), (0, 0)))

    def picked(rows):
        halves = rows.reshape(2, WAYS, count, *rows.shape[1:])
        return lax.dynamic_index_in_dim(halves, seq % 2, 0, keepdims=False)

    def tiled(block):
        return jnp.pad(block, ((0, 0), (0, ROWS - block.shape[1]), (0, CHUNK - block.shape[2])))

    rates_p, residues_p, gain_p = picked(log_rates), picked(residues), picked(skip_gain)
    pars = jnp.concatenate(
        [
            tiled(rates_p.transpose(0, 2, 1)),
            tiled(residues_p.transpose(0, 2, 1)),
            tiled(jnp.tile(rates_p, (1, 1, 3))),
            tiled(residues_p),
            tiled(jnp.broadcast_to(gain_p[:, :, None], (*gain_p.shape, CHUNK))),
        ],
        axis=1,
    )
    anywhere = pl.BlockSpec(memory_space=pl.ANY)
    vmem = pl.BlockSpec(memory_space=pltpu.VMEM)
    dma = pltpu.SemaphoreType.DMA
    tokens = SHARDS * CHUNK
    chunked = pltpu.VMEM((SHARDS, ROWS, CHUNK), F32)
    wgrad, shared = pl.pallas_call(
        functools.partial(kernel, count),
        out_shape=(
            jax.ShapeDtypeStruct((WAYS * TRIO, width), F32),
            jax.ShapeDtypeStruct((2 * WAYS, ROWS, CHUNK), F32),
        ),
        in_specs=[anywhere, anywhere, vmem, vmem],
        out_specs=(vmem, vmem),
        scratch_shapes=[
            pltpu.VMEM((SHARDS, CHUNK, width), BF16),
            pltpu.VMEM((WAYS * TRIO, width), BF16),
            pltpu.VMEM((SHARDS, WAYS, TRIO, CHUNK), BF16),
            pltpu.VMEM((WAYS, SHARDS, TRIO, CHUNK), BF16),
            pltpu.VMEM((SHARDS, ROWS, CHUNK), BF16),
            pltpu.VMEM((PARAM_ROWS, CHUNK), F32),
            chunked,
            chunked,
            chunked,
            pltpu.VMEM((SHARDS, TRIO, CHUNK), BF16),
            chunked,
            chunked,
            pltpu.VMEM((ROWS, CHUNK), F32),
            pltpu.VMEM((WAYS, TRIO, tokens), BF16),
            dma((2,)),
            dma((2, 22)),
            dma((2, 22)),
            dma((WAYS,)),
            dma((WAYS,)),
            dma((SHARDS,)),
            dma,
            dma((WAYS,)),
            dma,
            dma((9,)),
            dma((9,)),
            dma((SHARDS,)),
            dma,
        ],
        compiler_params=pltpu.CompilerParams(
            collective_id=0, has_side_effects=True, vmem_limit_bytes=48 * 2**20
        ),
    )(features, weight, grads, pars)
    weight_grad = wgrad.reshape(WAYS, 3, ROWS, width)[:, :, :count].transpose(0, 2, 1, 3)
    weight_grad = weight_grad.reshape(qkv_weight.shape)
    small = shared[:, :count].reshape(residues.shape[0], CHUNK)
    order = residues.shape[1]
    moment = small[:, order : 2 * order] + small[:, 2 * order : 3 * order]
    rate_grad = -residues * jnp.exp(log_rates) * moment
    return weight_grad, small[:, :order], rate_grad, small[:, 3 * order]


def solution(mesh):
    placed = (
        P("seq", "ch"),
        P("seq", None, "ch"),
        P("ch", "seq"),
        P("ch", None),
        P("ch", None),
        P("ch"),
    )
    return jax.shard_map(
        local,
        mesh=mesh,
        in_specs=placed,
        out_specs=(P("seq", None, "ch"), P("ch", None), P("ch", None), P("ch")),
        check_vma=False,
    )
```

```python
import functools

import jax
import jax.numpy as jnp
from jax import lax
from jax.experimental import pallas as pl
from jax.experimental.pallas import tpu as pltpu
from jax.sharding import PartitionSpec as P

F32, BF16 = jnp.float32, jnp.bfloat16
CHUNK = 128
SIDE = 4
SHARDS = SIDE * SIDE
WAYS = 2 * SIDE
ROWS = 16
TRIO = 40
STATE = 16
MESH = pl.DeviceIdType.MESH
PARAM_ROWS = 40

NT = (((1,), (1,)), ((), ()))
TN = (((0,), (0,)), ((), ()))
NN = (((1,), (0,)), ((), ()))


def mul(a, b, dims=NN):
    return lax.dot_general(a, b, dims, preferred_element_type=F32)


def exact(a, b, dims=NN):
    return lax.dot_general(a, b, dims, precision="highest", preferred_element_type=F32)


def iota(shape, dim):
    return lax.broadcasted_iota(jnp.int32, shape, dim)


def chosen(shape, rule, kind=BF16):
    return rule(iota(shape, 0), iota(shape, 1)).astype(kind)


def sum_partials(parts, grads, projf, projr, gradf):
    flip = chosen((CHUNK, CHUNK), lambda r, c: r + c == CHUNK - 1)

    def body(k, _):
        total = parts[0, k].astype(F32)
        for way in range(1, WAYS):
            total = total + parts[way, k].astype(F32)
        rounded = total.astype(BF16)
        projf[k] = rounded.astype(F32)
        projr[k] = mul(rounded, flip)
        gradf[k] = grads[k].astype(F32)
        return 0

    lax.fori_loop(0, SHARDS, body, 0, unroll=4)


def carry(values, step, lagged, reverse):
    row = iota(values.shape, 0)
    shape = values.shape
    decay = jnp.broadcast_to(step, shape)
    reach = 1
    while reach < shape[0]:
        amount = shape[0] - reach if reverse else reach
        keep = row < shape[0] - reach if reverse else row >= reach
        near = jnp.where(keep, decay * pltpu.roll(values, amount, 0), 0.0)
        if lagged is not None:
            moved = jnp.where(keep, decay * pltpu.roll(lagged, amount, 0), 0.0)
            lagged = lagged + moved + (CHUNK * reach) * near
        values = values + near
        decay = decay * decay
        reach *= 2
    return values, lagged


def before(values, reverse):
    row = iota(values.shape, 0)
    last = values.shape[0] - 1
    if reverse:
        return jnp.where(row < last, pltpu.roll(values, last, 0), 0.0)
    return jnp.where(row >= 1, pltpu.roll(values, 1, 0), 0.0)


def select_params(count, offset, params, cols, rows, gains):
    lanes = params.shape[1]
    down = chosen((lanes, CHUNK), lambda r, c: (r == c + offset) & (c < count), F32)
    across = chosen((ROWS, lanes), lambda r, c: (c == r + offset) & (r < count), F32)
    cols[...] = exact(params[0 : 2 * STATE], down)
    rates = params[0:STATE]
    rows[:, 0 : 3 * STATE] = exact(across, jnp.concatenate([rates, rates, rates], 0), NT)
    gain = jnp.broadcast_to(params[2 * STATE : 2 * STATE + 1], (CHUNK, lanes))
    gains[...] = exact(across, gain, NT)


def tables_of(c, cols, bands, tables):
    lane = iota((STATE, CHUNK), 1).astype(F32)
    rates = jnp.exp(cols[0:STATE, c : c + 1])
    residues = cols[STATE : 2 * STATE, c : c + 1]
    near = jnp.exp(-rates * lane)
    far = jnp.exp(-rates * (CHUNK - lane))
    weighted = residues * near
    taps = jnp.sum(weighted, axis=0, keepdims=True)
    upper = iota((CHUNK, CHUNK), 1) >= iota((CHUNK, CHUNK), 0)
    spread = pltpu.roll(jnp.broadcast_to(taps, (CHUNK, CHUNK)), 0, 1, stride=1, stride_axis=0)
    bands[c] = jnp.where(upper, spread, 0.0).astype(BF16)
    far_lag = (far * (CHUNK - lane)).astype(BF16)
    blocks = [near, near * lane, near, far, far, far, None, None, None, weighted, residues * far]
    for at, block in enumerate(blocks):
        tables[c, at * STATE : (at + 1) * STATE] = far_lag if block is None else block.astype(BF16)


def mix_channels(group, rows, gains, bands, tables, projf, projr, gradf, small, skips, outs):
    lower = iota((CHUNK, CHUNK), 1) <= iota((CHUNK, CHUNK), 0)
    third = iota((SHARDS, 3 * STATE), 1) < 2 * STATE
    kvs, gms, firsts = {}, {}, {}
    for c in group:
        kv = projf[:, 3 * c + 1, :] * projf[:, 3 * c + 2, :]
        gm = gradf[:, c, :] * projf[:, 3 * c, :]
        back = projr[:, 3 * c + 1, :] * projr[:, 3 * c + 2, :]
        kvs[c], gms[c] = kv, gm
        skips[c : c + 1] = jnp.sum(kv * gm, axis=0, keepdims=True)
        kv, gm, back = kv.astype(BF16), gm.astype(BF16), back.astype(BF16)
        firsts[c] = (
            mul(kv, tables[c, 3 * STATE : 6 * STATE], NT),
            mul(kv, tables[c, 6 * STATE : 9 * STATE], NT),
            mul(gm, tables[c, 0 : 3 * STATE], NT),
            mul(back, gm, TN),
            mul(kv, bands[c]),
            mul(gm, bands[c], NT),
        )
    seconds = {}
    for c in group:
        tails, tails_lag, heads, product, _, _ = firsts[c]
        step = jnp.exp(-CHUNK * jnp.exp(rows[c : c + 1, 0 : 3 * STATE]))
        states, states_lag = carry(tails, step, tails_lag, False)
        states, states_lag = before(states, False), before(states_lag, False)
        inter = jnp.sum(heads * jnp.where(third, states, states_lag), axis=0, keepdims=True)
        adjoints, _ = carry(heads[:, 0:STATE], step[:, 0:STATE], None, True)
        adjoints = before(adjoints, True)
        skewed = pltpu.roll(product, 1, 1, stride=1, stride_axis=0)
        sums = jnp.sum(jnp.where(lower, skewed, 0.0), axis=0, keepdims=True)
        wide = jnp.broadcast_to(sums, (ROWS, CHUNK)).astype(BF16)
        seconds[c] = (
            mul(states[:, 0:STATE].astype(BF16), tables[c, 9 * STATE : 10 * STATE]),
            mul(adjoints.astype(BF16), tables[c, 10 * STATE : 11 * STATE]),
            mul(wide, tables[c, 0 : 2 * STATE], NT),
            inter,
        )
    for c in group:
        conv, corr, intra, inter = seconds[c]
        gain = gains[c : c + 1]
        conv = conv + firsts[c][4] + gain * kvs[c]
        grad_mix = corr + firsts[c][5] + gain * gms[c]
        outs[:, 3 * c, :] = gradf[:, c, :] * conv
        outs[:, 3 * c + 1, :] = grad_mix * projf[:, 3 * c + 2, :]
        outs[:, 3 * c + 2, :] = grad_mix * projf[:, 3 * c + 1, :]
        small[c : c + 1, 0 : 3 * STATE] = inter
        small[c : c + 1, 0 : 2 * STATE] += intra[0:1]


def pack(outs, mine, first, last):
    for k in range(SHARDS):
        mine[first:last, k * CHUNK : (k + 1) * CHUNK] = outs[k, first:last].astype(BF16)


def finish_small(count, small, skips):
    lane = iota((ROWS, CHUNK), 1)
    row = iota((ROWS, CHUNK), 0)
    summed = jnp.sum(skips[...], axis=1, keepdims=True)
    filled = jnp.where(lane == 3 * STATE, summed, small[...])
    small[...] = jnp.where(row < count, filled, 0.0)


def kernel(
    count, feat, weight, gout, rates_t, residues_t, gain, wgrad, residue_out, rate_out, skip_out,
    every, wraw, wbuf, graw, gbuf, packed, partial, parts, grads, params, cols, rows, gains, bands,
    tables, projf, projr, gradf, outs, small, skips, shared, full, ordered_grads,
    local_sem, f_send, f_recv, r_send, r_recv, g_send, g_recv, p_send, p_recv, a_send, a_recv,
    s_send, s_recv,
):
    seq, ch = lax.axis_index("seq"), lax.axis_index("ch")
    x, z = seq // SIDE, seq % SIDE
    y, core = ch // 2, ch % 2
    home = seq // 2
    at_home = ch == home

    feat_in = pltpu.make_async_copy(feat, every.at[seq], local_sem.at[0])
    weight_in = pltpu.make_async_copy(weight, wraw, local_sem.at[1])
    grads_in = pltpu.make_async_copy(gout, graw, local_sem.at[2])
    small_in = [
        pltpu.make_async_copy(rates_t, packed.at[pl.ds(0, STATE)], local_sem.at[3]),
        pltpu.make_async_copy(residues_t, packed.at[pl.ds(STATE, STATE)], local_sem.at[4]),
        pltpu.make_async_copy(gain, packed.at[pl.ds(2 * STATE, 8)], local_sem.at[5]),
    ]
    feat_in.start()
    for copy in small_in:
        copy.start()
    weight_in.start()
    grads_in.start()

    def ring(value, step):
        return (value + step + SIDE) % SIDE

    def place(v, p, q):
        return p * SIDE + q if v == 0 else q * SIDE + p

    def spot(v):
        return (x, z) if v == 0 else (z, x)

    barrier = pltpu.get_barrier_semaphore()

    def greet(s, c):
        pl.semaphore_signal(barrier, inc=1, device_id={"seq": s, "ch": c}, device_id_type=MESH)

    for v in range(2):
        p, q = spot(v)
        for step in (-1, 1):
            greet(place(v, ring(p, step), q), ch)
    for i in range(1, WAYS):
        greet(seq, (ch + i) % WAYS)
    small[...] = jnp.zeros_like(small)
    skips[...] = jnp.zeros_like(skips)
    outs[:, TRIO - 1, :] = jnp.zeros((SHARDS, CHUNK), F32)
    pl.semaphore_wait(barrier, 4 + WAYS - 1)

    half, quarter = CHUNK // 2, CHUNK // 4
    offs = (0, -1, 1, 2)

    def piece(v, part):
        start = v * half + (quarter if part == "b" else 0)
        return pl.ds(start, half if part == "h" else quarter)

    names = [("P1+", "h"), ("P1-", "h"), ("P2+", "a"), ("P2-", "b")]
    for j in range(3):
        names += [(f"Q1+{j}", "h"), (f"Q1-{j}", "h"), (f"Q2+{j}", "a"), (f"Q2-{j}", "b")]
    names += [("Q1+3a", "a"), ("Q1+3b", "b"), ("Q1-3a", "a"), ("Q1-3b", "b")]
    names += [("Q2+3", "a"), ("Q2-3", "b")]
    number = {name: n for n, (name, _) in enumerate(names)}
    piece_of = dict(names)

    def feature_copy(v, name, arriving):
        p, q = spot(v)
        step = 1 if name[2] == "+" else -1
        hops = int(name[1]) - 1 + (1 if arriving else 0)
        if name[0] == "P":
            source = place(v, ring(p, -step * hops), q)
            target = place(v, ring(p, step), q)
        else:
            source = place(v, ring(p, offs[int(name[3])]), ring(q, -step * hops))
            target = place(v, p, ring(q, step))
        rows = piece(v, piece_of[name])
        return pltpu.make_async_remote_copy(
            src_ref=every.at[source, rows],
            dst_ref=every.at[source, rows],
            send_sem=f_send.at[v, number[name]],
            recv_sem=f_recv.at[v, number[name]],
            device_id={"seq": target},
            device_id_type=MESH,
        )

    def send(v, name):
        feature_copy(v, name, False).start()

    def arrive(v, name):
        feature_copy(v, name, True).wait_recv()

    def owner_copy(shard, i):
        target = (ch + i) % WAYS
        return pltpu.make_async_remote_copy(
            src_ref=partial.at[shard, target],
            dst_ref=parts.at[i, shard],
            send_sem=r_send.at[i],
            recv_sem=r_recv.at[i],
            device_id={"ch": target},
            device_id_type=MESH,
        )

    def shard_at(dx, dz):
        return ring(x, dx) * SIDE + ring(z, dz)

    def project(dx, dz):
        shard = shard_at(dx, dz)
        out = mul(wbuf[...], every[shard], NT).astype(BF16).reshape(WAYS, TRIO, CHUNK)
        partial[shard] = out
        parts[0, shard] = partial[shard, ch]
        return shard

    def deliver(shard):
        for i in range(1, WAYS):
            owner_copy(shard, i).start()

    feat_in.wait()
    for v in range(2):
        send(v, "P1+")
        send(v, "P1-")
    for v in range(2):
        send(v, "Q1+0")
        send(v, "Q1-0")

    def param_copy(i):
        return pltpu.make_async_remote_copy(
            src_ref=packed,
            dst_ref=params,
            send_sem=p_send.at[i],
            recv_sem=p_recv,
            device_id={"ch": (ch + i) % WAYS},
            device_id_type=MESH,
        )

    for copy in small_in:
        copy.wait()

    @pl.when(at_home)
    def _():
        pltpu.make_async_copy(packed, params, p_recv).start()
        for i in range(1, WAYS):
            param_copy(i).start()

    def grad_copy(shard, c):
        slot = (shard % 2) * WAYS + c
        return pltpu.make_async_remote_copy(
            src_ref=gbuf.at[slot],
            dst_ref=grads.at[seq],
            send_sem=g_send.at[slot],
            recv_sem=g_recv,
            device_id={"seq": shard, "ch": c},
            device_id_type=MESH,
        )

    def give_grads(dx, dz):
        shard = shard_at(dx, dz)

        @pl.when(shard // 2 == ch)
        def _():
            def one(c, _):
                if dx or dz:
                    grad_copy(shard, c).start()
                else:
                    @pl.when(c == ch)
                    def _():
                        slot = (shard % 2) * WAYS + c
                        pltpu.make_async_copy(gbuf.at[slot], grads.at[seq], g_recv).start()

                    @pl.when(c != ch)
                    def _():
                        grad_copy(shard, c).start()

                return 0

            lax.fori_loop(0, WAYS, one, 0)

    weight_in.wait()
    block = count * WAYS
    ordered = None
    for g in range(3):
        pick = chosen(
            (WAYS * TRIO, block),
            lambda r, c: (r % TRIO == 3 * (c % count) + g) & (r // TRIO == c // count),
        )
        part = mul(pick, wraw[g])
        ordered = part if ordered is None else ordered + part
    wbuf[...] = ordered.astype(BF16)
    grads_in.wait()
    pick = chosen(
        (2 * WAYS * ROWS, 2 * block), lambda r, c: (r // ROWS == c // count) & (r % ROWS == c % count)
    )
    gbuf[...] = mul(pick, graw[...]).astype(BF16).reshape(2 * WAYS, ROWS, CHUNK)

    done = [project(0, 0)]
    give_grads(0, 0)

    def follow(dx, dz):
        done.append(project(dx, dz))
        deliver(done[-2])

    prepared = []

    def prepare(number_of):
        for _ in range(number_of):
            if len(prepared) < count:
                tables_of(len(prepared), cols, bands, tables)
                prepared.append(0)

    for v in range(2):
        near = ((-1, 0), (1, 0)) if v == 0 else ((0, -1), (0, 1))
        arrive(v, "P1+")
        send(v, "P2+")
        send(v, "Q1+1")
        send(v, "Q1-1")
        give_grads(*near[0])
        arrive(v, "P1-")
        send(v, "P2-")
        send(v, "Q1+2")
        send(v, "Q1-2")
        give_grads(*near[1])
    pltpu.make_async_copy(packed, params, p_recv).wait()
    for v in range(2):
        arrive(v, "Q1+0")
        send(v, "Q2+0")
        arrive(v, "Q1-0")
        send(v, "Q2-0")
    offset = (seq % 2) * block + ch * count
    select_params(count, offset, params, cols, rows, gains)
    for v in range(2):
        arrive(v, "P2+")
        send(v, "Q1+3a")
        send(v, "Q1-3a")
        arrive(v, "P2-")
        send(v, "Q1+3b")
        send(v, "Q1-3b")
        give_grads(*((2, 0) if v == 0 else (0, 2)))
    for dx, dz in ((-1, 0), (1, 0), (0, -1), (0, 1)):
        follow(dx, dz)
    prepare(2)
    for j in (1, 2):
        for v in range(2):
            arrive(v, f"Q1+{j}")
            send(v, f"Q2+{j}")
            arrive(v, f"Q1-{j}")
            send(v, f"Q2-{j}")
        give_grads(-1 if j == 1 else 1, -1)
        give_grads(-1 if j == 1 else 1, 1)
        prepare(2)
    for dx, dz in ((-1, -1), (-1, 1), (1, -1), (1, 1)):
        follow(dx, dz)
        prepare(1)
    for v in range(2):
        arrive(v, "Q1+3a")
        send(v, "Q2+3")
        arrive(v, "Q1-3b")
        send(v, "Q2-3")
        for side in (-1, 1):
            give_grads(*((2, side) if v == 0 else (side, 2)))
    for v in range(2):
        arrive(v, "Q1+3b")
        arrive(v, "Q1-3a")
        arrive(v, "Q2+0")
        arrive(v, "Q2-0")
    for dx, dz in ((2, 0), (0, 2)):
        follow(dx, dz)
        prepare(1)
    for v in range(2):
        for j in (1, 2):
            arrive(v, f"Q2+{j}")
            arrive(v, f"Q2-{j}")
    for dx, dz in ((2, -1), (2, 1), (-1, 2), (1, 2)):
        follow(dx, dz)
    for v in range(2):
        arrive(v, "Q2+3")
        arrive(v, "Q2-3")
    give_grads(2, 2)
    follow(2, 2)
    deliver(done[-1])
    prepare(count)

    pltpu.make_async_copy(gbuf, grads, g_recv).wait()
    for i in range(1, WAYS):
        pltpu.make_async_copy(parts.at[0], parts.at[i], r_recv.at[i]).wait()
    sum_partials(parts, grads, projf, projr, gradf)

    width = SHARDS * CHUNK
    left, right = pl.ds(0, width // 2), pl.ds(width // 2, width // 2)
    whole = pl.ds(0, width)
    tiles = [pl.ds(0, 16), pl.ds(16, 16), pl.ds(32, TRIO - 32)]

    def owner(step, other):
        return ring(y, step) * 2 + (1 - core if other else core)

    def group_copy(t, n, slot, target, lanes):
        return pltpu.make_async_remote_copy(
            src_ref=full.at[slot, tiles[t], lanes],
            dst_ref=full.at[slot, tiles[t], lanes],
            send_sem=a_send.at[t, n],
            recv_sem=a_recv.at[t, n],
            device_id={"ch": target},
            device_id_type=MESH,
        )

    kinds = [
        (0, 1, False, whole),
        (0, -1, False, whole),
        (0, 0, True, whole),
        (1, 1, False, left),
        (-1, -1, False, right),
        (1, 0, True, whole),
        (-1, 0, True, whole),
        (2, 0, True, left),
        (2, 0, True, right),
    ]

    def going(t, n):
        back, step, other, lanes = kinds[n]
        return group_copy(t, n, owner(-back, False), owner(step, other), lanes)

    def coming(t, n):
        back, step, other, lanes = kinds[n]
        return group_copy(t, n, owner(-back - step, other), owner(step, other), lanes)

    def begin(t):
        for n in (0, 1, 2):
            going(t, n).start()

    def relay(t):
        coming(t, 0).wait_recv()
        going(t, 3).start()
        going(t, 5).start()
        coming(t, 1).wait_recv()
        going(t, 4).start()
        going(t, 6).start()

    def relay_far(t):
        coming(t, 3).wait_recv()
        going(t, 7).start()
        coming(t, 4).wait_recv()
        going(t, 8).start()

    mine = full.at[ch]
    groups = [range(0, 6), range(6, 11), range(11, count)]
    edges = [(0, 16), (16, 32), (32, TRIO)]
    for t in range(3):
        mix_channels(
            groups[t], rows, gains, bands, tables, projf, projr, gradf, small, skips, outs
        )
        pack(outs, mine, *edges[t])
        begin(t)
        if t > 0:
            relay(t - 1)
    finish_small(count, small, skips)

    def small_copy(i):
        return pltpu.make_async_remote_copy(
            src_ref=small,
            dst_ref=shared.at[(seq % 2) * WAYS + ch],
            send_sem=s_send.at[i],
            recv_sem=s_recv,
            device_id={"seq": i, "ch": home},
            device_id_type=MESH,
        )

    def small_self(i):
        return jnp.logical_and(i == seq, at_home)

    def start_small(i, _):
        @pl.when(small_self(i))
        def _():
            pltpu.make_async_copy(small, shared.at[(seq % 2) * WAYS + ch], s_recv).start()

        @pl.when(jnp.logical_not(small_self(i)))
        def _():
            small_copy(i).start()

        return 0

    relay_far(0)
    lax.fori_loop(0, SHARDS, start_small, 0)
    relay_far(1)
    relay(2)
    relay_far(2)

    pltpu.make_async_copy(shared, shared, s_recv).wait()
    pick = chosen(
        (2 * WAYS * ROWS, 2 * block),
        lambda r, c: (r // ROWS == c // count) & (r % ROWS == c % count),
        F32,
    )
    turned = exact(shared[...].reshape(2 * WAYS * ROWS, CHUNK), pick, TN)
    moment = turned[STATE : 2 * STATE] + turned[2 * STATE : 3 * STATE]
    residue_out[...] = turned[0:STATE]
    rate_out[...] = -packed[STATE : 2 * STATE] * jnp.exp(packed[0:STATE]) * moment
    skip_out[...] = turned[3 * STATE : 3 * STATE + 1]

    for t in range(3):
        for n in (2, 5, 6, 7, 8):
            coming(t, n).wait_recv()

    tile = 256
    gathered = full[...].reshape(WAYS * TRIO, width)
    sides = []
    for g in range(3):
        pick = chosen(
            (block, WAYS * TRIO),
            lambda r, c: (c % TRIO == 3 * (r % count) + g) & (c // TRIO == r // count),
        )
        sides.append(mul(pick, gathered).astype(BF16))
    for g in range(3):
        ordered_grads[g] = sides[g]

    def weight_columns(n, _):
        lanes = pl.ds(pl.multiple_of(n * tile, tile), tile)
        right_side = every[:, :, lanes].reshape(width, tile)
        for g in range(3):
            wgrad[g, :, lanes] = mul(ordered_grads[g], right_side)
        return 0

    lax.fori_loop(0, every.shape[2] // tile, weight_columns, 0)

    for t in range(3):
        for n in range(9):
            going(t, n).wait_send()
    for v in range(2):
        for name, _ in names:
            feature_copy(v, name, False).wait_send()
    for i in range(1, WAYS):
        pltpu.make_async_copy(parts.at[0], parts.at[i], r_send.at[i]).wait()

    def end_small(i, _):
        shard = 2 * ch + i // WAYS

        @pl.when(jnp.logical_not(jnp.logical_and(shard == seq, i % WAYS == ch)))
        def _():
            grad_copy(shard, i % WAYS).wait_send()

        @pl.when(jnp.logical_not(small_self(i)))
        def _():
            small_copy(i).wait_send()

        return 0

    lax.fori_loop(0, SHARDS, end_small, 0)

    @pl.when(at_home)
    def _():
        for i in range(1, WAYS):
            param_copy(i).wait_send()


def local(features, qkv_weight, grad_out, residues, log_rates, skip_gain):
    width = features.shape[1]
    block = qkv_weight.shape[0]
    count = block // WAYS
    held, order = residues.shape
    weight = qkv_weight.transpose(1, 0, 2)
    gain = jnp.broadcast_to(skip_gain[None], (8, held))
    anywhere = pl.BlockSpec(memory_space=pl.ANY)
    vmem = pl.BlockSpec(memory_space=pltpu.VMEM)
    dma = pltpu.SemaphoreType.DMA
    tokens = SHARDS * CHUNK
    weight_grad, residue_grad, rate_grad, skip_grad = pl.pallas_call(
        functools.partial(kernel, count),
        out_shape=(
            jax.ShapeDtypeStruct((3, block, width), F32),
            jax.ShapeDtypeStruct((order, held), F32),
            jax.ShapeDtypeStruct((order, held), F32),
            jax.ShapeDtypeStruct((1, held), F32),
        ),
        in_specs=[anywhere] * 6,
        out_specs=(vmem,) * 4,
        scratch_shapes=[
            pltpu.VMEM((SHARDS, CHUNK, width), BF16),
            pltpu.VMEM((3, block, width), BF16),
            pltpu.VMEM((WAYS * TRIO, width), BF16),
            pltpu.VMEM((held, CHUNK), BF16),
            pltpu.VMEM((2 * WAYS, ROWS, CHUNK), BF16),
            pltpu.VMEM((PARAM_ROWS, held), F32),
            pltpu.VMEM((SHARDS, WAYS, TRIO, CHUNK), BF16),
            pltpu.VMEM((WAYS, SHARDS, TRIO, CHUNK), BF16),
            pltpu.VMEM((SHARDS, ROWS, CHUNK), BF16),
            pltpu.VMEM((PARAM_ROWS, held), F32),
            pltpu.VMEM((2 * STATE, CHUNK), F32),
            pltpu.VMEM((ROWS, CHUNK), F32),
            pltpu.VMEM((ROWS, CHUNK), F32),
            pltpu.VMEM((ROWS, CHUNK, CHUNK), BF16),
            pltpu.VMEM((ROWS, 11 * STATE, CHUNK), BF16),
            pltpu.VMEM((SHARDS, TRIO, CHUNK), F32),
            pltpu.VMEM((SHARDS, TRIO, CHUNK), F32),
            pltpu.VMEM((SHARDS, ROWS, CHUNK), F32),
            pltpu.VMEM((SHARDS, TRIO, CHUNK), F32),
            pltpu.VMEM((ROWS, CHUNK), F32),
            pltpu.VMEM((ROWS, CHUNK), F32),
            pltpu.VMEM((2 * WAYS, ROWS, CHUNK), F32),
            pltpu.VMEM((WAYS, TRIO, tokens), BF16),
            pltpu.VMEM((3, block, tokens), BF16),
            dma((6,)),
            dma((2, 22)),
            dma((2, 22)),
            dma((WAYS,)),
            dma((WAYS,)),
            dma((SHARDS,)),
            dma,
            dma((WAYS,)),
            dma,
            dma((3, 9)),
            dma((3, 9)),
            dma((SHARDS,)),
            dma,
        ],
        compiler_params=pltpu.CompilerParams(
            collective_id=0, has_side_effects=True, vmem_limit_bytes=48 * 2**20
        ),
    )(features, weight, grad_out, log_rates.T, residues.T, gain)
    return weight_grad.transpose(1, 0, 2), residue_grad.T, rate_grad.T, skip_grad.reshape(held)


def solution(mesh):
    placed = (
        P("seq", "ch"),
        P("seq", None, "ch"),
        P("ch", "seq"),
        P("ch", None),
        P("ch", None),
        P("ch"),
    )
    return jax.shard_map(
        local,
        mesh=mesh,
        in_specs=placed,
        out_specs=(P("seq", None, "ch"), P("ch", None), P("ch", None), P("ch")),
        check_vma=False,
    )
```

```python
import functools

import jax
import jax.numpy as jnp
from jax import lax
from jax.experimental import pallas as pl
from jax.experimental.pallas import tpu as pltpu
from jax.sharding import PartitionSpec as P

F32, BF16 = jnp.float32, jnp.bfloat16
CHUNK = 128
SIDE = 4
SHARDS = SIDE * SIDE
WAYS = 2 * SIDE
ROWS = 16
TRIO = 40
STATE = 16
MESH = pl.DeviceIdType.MESH
PARAM_ROWS = 2 * STATE

NT = (((1,), (1,)), ((), ()))
TN = (((0,), (0,)), ((), ()))
NN = (((1,), (0,)), ((), ()))


def mul(a, b, dims=NN):
    return lax.dot_general(a, b, dims, preferred_element_type=F32)


def exact(a, b, dims=NN):
    return lax.dot_general(a, b, dims, precision="highest", preferred_element_type=F32)


def iota(shape, dim):
    return lax.broadcasted_iota(jnp.int32, shape, dim)


def chosen(shape, rule, kind=BF16):
    return rule(iota(shape, 0), iota(shape, 1)).astype(kind)


def sum_partials(parts, grads, projf, projr, gradf):
    flip = chosen((CHUNK, CHUNK), lambda r, c: r + c == CHUNK - 1)

    def body(k, _):
        total = parts[0, k].astype(F32)
        for way in range(1, WAYS):
            total = total + parts[way, k].astype(F32)
        rounded = total.astype(BF16)
        projf[k] = rounded.astype(F32)
        projr[k] = mul(rounded, flip)
        gradf[k] = grads[k].astype(F32)
        return 0

    lax.fori_loop(0, SHARDS, body, 0, unroll=4)


def carry(values, step, lagged, reverse):
    row = iota(values.shape, 0)
    shape = values.shape
    decay = jnp.broadcast_to(step, shape)
    reach = 1
    while reach < shape[0]:
        amount = shape[0] - reach if reverse else reach
        keep = row < shape[0] - reach if reverse else row >= reach
        near = jnp.where(keep, decay * pltpu.roll(values, amount, 0), 0.0)
        if lagged is not None:
            moved = jnp.where(keep, decay * pltpu.roll(lagged, amount, 0), 0.0)
            lagged = lagged + moved + (CHUNK * reach) * near
        values = values + near
        decay = decay * decay
        reach *= 2
    return values, lagged


def before(values, reverse):
    row = iota(values.shape, 0)
    last = values.shape[0] - 1
    if reverse:
        return jnp.where(row < last, pltpu.roll(values, last, 0), 0.0)
    return jnp.where(row >= 1, pltpu.roll(values, 1, 0), 0.0)


def select_params(count, offset, params, gain, cols, rows, gains):
    lanes = params.shape[1]
    down = chosen((lanes, CHUNK), lambda r, c: (r == c + offset) & (c < count), F32)
    across = chosen((ROWS, lanes), lambda r, c: (c == r + offset) & (r < count), F32)
    cols[...] = exact(params[0 : 2 * STATE], down)
    rates = params[0:STATE]
    rows[:, 0 : 3 * STATE] = exact(across, jnp.concatenate([rates, rates, rates], 0), NT)
    gains[...] = exact(across, jnp.broadcast_to(gain[...], (CHUNK, lanes)), NT)


def tables_of(c, cols, bands, tables):
    lane = iota((STATE, CHUNK), 1).astype(F32)
    rates = jnp.exp(cols[0:STATE, c : c + 1])
    residues = cols[STATE : 2 * STATE, c : c + 1]
    near = jnp.exp(-rates * lane)
    far = jnp.exp(-rates * (CHUNK - lane))
    weighted = residues * near
    taps = jnp.sum(weighted, axis=0, keepdims=True)
    upper = iota((CHUNK, CHUNK), 1) >= iota((CHUNK, CHUNK), 0)
    spread = pltpu.roll(jnp.broadcast_to(taps, (CHUNK, CHUNK)), 0, 1, stride=1, stride_axis=0)
    bands[c] = jnp.where(upper, spread, 0.0).astype(BF16)
    far_lag = (far * (CHUNK - lane)).astype(BF16)
    blocks = [near, near * lane, near, far, far, far, None, None, None, weighted, residues * far]
    for at, block in enumerate(blocks):
        tables[c, at * STATE : (at + 1) * STATE] = far_lag if block is None else block.astype(BF16)


def mix_channels(group, rows, gains, bands, tables, projf, projr, gradf, small, skips, outs):
    lower = iota((CHUNK, CHUNK), 1) <= iota((CHUNK, CHUNK), 0)
    third = iota((SHARDS, 3 * STATE), 1) < 2 * STATE
    kvs, gms, firsts = {}, {}, {}
    for c in group:
        kv = projf[:, 3 * c + 1, :] * projf[:, 3 * c + 2, :]
        gm = gradf[:, c, :] * projf[:, 3 * c, :]
        back = projr[:, 3 * c + 1, :] * projr[:, 3 * c + 2, :]
        kvs[c], gms[c] = kv, gm
        skips[c : c + 1] = jnp.sum(kv * gm, axis=0, keepdims=True)
        kv, gm, back = kv.astype(BF16), gm.astype(BF16), back.astype(BF16)
        firsts[c] = (
            mul(kv, tables[c, 3 * STATE : 6 * STATE], NT),
            mul(kv, tables[c, 6 * STATE : 9 * STATE], NT),
            mul(gm, tables[c, 0 : 3 * STATE], NT),
            mul(back, gm, TN),
            mul(kv, bands[c]),
            mul(gm, bands[c], NT),
        )
    seconds = {}
    for c in group:
        tails, tails_lag, heads, product, _, _ = firsts[c]
        step = jnp.exp(-CHUNK * jnp.exp(rows[c : c + 1, 0 : 3 * STATE]))
        states, states_lag = carry(tails, step, tails_lag, False)
        states, states_lag = before(states, False), before(states_lag, False)
        inter = jnp.sum(heads * jnp.where(third, states, states_lag), axis=0, keepdims=True)
        adjoints, _ = carry(heads[:, 0:STATE], step[:, 0:STATE], None, True)
        adjoints = before(adjoints, True)
        skewed = pltpu.roll(product, 1, 1, stride=1, stride_axis=0)
        sums = jnp.sum(jnp.where(lower, skewed, 0.0), axis=0, keepdims=True)
        wide = jnp.broadcast_to(sums, (ROWS, CHUNK)).astype(BF16)
        seconds[c] = (
            mul(states[:, 0:STATE].astype(BF16), tables[c, 9 * STATE : 10 * STATE]),
            mul(adjoints.astype(BF16), tables[c, 10 * STATE : 11 * STATE]),
            mul(wide, tables[c, 0 : 2 * STATE], NT),
            inter,
        )
    for c in group:
        conv, corr, intra, inter = seconds[c]
        gain = gains[c : c + 1]
        conv = conv + firsts[c][4] + gain * kvs[c]
        grad_mix = corr + firsts[c][5] + gain * gms[c]
        outs[:, 3 * c, :] = gradf[:, c, :] * conv
        outs[:, 3 * c + 1, :] = grad_mix * projf[:, 3 * c + 2, :]
        outs[:, 3 * c + 2, :] = grad_mix * projf[:, 3 * c + 1, :]
        small[c : c + 1, 0 : 3 * STATE] = inter
        small[c : c + 1, 0 : 2 * STATE] += intra[0:1]


def pack(outs, mine, first, last):
    for k in range(SHARDS):
        mine[first:last, k * CHUNK : (k + 1) * CHUNK] = outs[k, first:last].astype(BF16)


def finish_small(count, small, skips):
    lane = iota((ROWS, CHUNK), 1)
    row = iota((ROWS, CHUNK), 0)
    summed = jnp.sum(skips[...], axis=1, keepdims=True)
    filled = jnp.where(lane == 3 * STATE, summed, small[...])
    small[...] = jnp.where(row < count, filled, 0.0)


def kernel(
    count, feat, weight, gout, rates_t, residues_t, gain, every, full, shared, packed,
    wraw, wbuf, graw, gbuf, partial, parts, grads, params, cols, rows, gains, bands,
    tables, projf, projr, gradf, outs, small, skips, gain_in, gain_got, mine,
    local_sem, f_send, f_recv, r_send, r_recv, g_send, g_recv, p_send, p_recv, a_send, a_recv,
    s_send, s_recv, hello, k_send, k_recv, store_sem,
):
    seq, ch = lax.axis_index("seq"), lax.axis_index("ch")
    x, z = seq // SIDE, seq % SIDE
    y, core = ch // 2, ch % 2
    home = seq // 2
    at_home = ch == home

    feat_in = pltpu.make_async_copy(feat, every.at[seq], local_sem.at[0])
    weight_in = pltpu.make_async_copy(weight, wraw, local_sem.at[1])
    grads_in = pltpu.make_async_copy(gout, graw, local_sem.at[2])
    small_in = [
        pltpu.make_async_copy(rates_t, packed.at[pl.ds(0, STATE)], local_sem.at[3]),
        pltpu.make_async_copy(residues_t, packed.at[pl.ds(STATE, STATE)], local_sem.at[4]),
        pltpu.make_async_copy(gain, gain_in, local_sem.at[5]),
    ]
    feat_in.start()
    for copy in small_in:
        copy.start()
    weight_in.start()
    grads_in.start()

    def ring(value, step):
        return (value + step + SIDE) % SIDE

    def place(v, p, q):
        return p * SIDE + q if v == 0 else q * SIDE + p

    def spot(v):
        return (x, z) if v == 0 else (z, x)

    barrier = pltpu.get_barrier_semaphore()

    def greet(s, c):
        pl.semaphore_signal(barrier, inc=1, device_id={"seq": s, "ch": c}, device_id_type=MESH)

    for v in range(2):
        p, q = spot(v)
        for step in (-1, 1):
            greet(place(v, ring(p, step), q), ch)
    for i in range(1, WAYS):
        greet(seq, (ch + i) % WAYS)
    small[...] = jnp.zeros_like(small)
    skips[...] = jnp.zeros_like(skips)
    outs[:, TRIO - 1, :] = jnp.zeros((SHARDS, CHUNK), F32)
    pl.semaphore_wait(barrier, 4 + WAYS - 1)

    half, quarter = CHUNK // 2, CHUNK // 4
    offs = (0, -1, 1, 2)

    def piece(v, part):
        start = v * half + (quarter if part == "b" else 0)
        return pl.ds(start, half if part == "h" else quarter)

    names = [("P1+", "h"), ("P1-", "h"), ("P2+", "a"), ("P2-", "b")]
    for j in range(3):
        names += [(f"Q1+{j}", "h"), (f"Q1-{j}", "h"), (f"Q2+{j}", "a"), (f"Q2-{j}", "b")]
    names += [("Q1+3a", "a"), ("Q1+3b", "b"), ("Q1-3a", "a"), ("Q1-3b", "b")]
    names += [("Q2+3", "a"), ("Q2-3", "b")]
    number = {name: n for n, (name, _) in enumerate(names)}
    piece_of = dict(names)

    def feature_copy(v, name, arriving):
        p, q = spot(v)
        step = 1 if name[2] == "+" else -1
        hops = int(name[1]) - 1 + (1 if arriving else 0)
        if name[0] == "P":
            source = place(v, ring(p, -step * hops), q)
            target = place(v, ring(p, step), q)
        else:
            source = place(v, ring(p, offs[int(name[3])]), ring(q, -step * hops))
            target = place(v, p, ring(q, step))
        rows = piece(v, piece_of[name])
        return pltpu.make_async_remote_copy(
            src_ref=every.at[source, rows],
            dst_ref=every.at[source, rows],
            send_sem=f_send.at[v, number[name]],
            recv_sem=f_recv.at[v, number[name]],
            device_id={"seq": target},
            device_id_type=MESH,
        )

    def send(v, name):
        feature_copy(v, name, False).start()

    def arrive(v, name):
        feature_copy(v, name, True).wait_recv()

    def hello_round(n):
        for v in range(2):
            p, q = spot(v)
            for step in (-1, 1):
                pl.semaphore_signal(
                    hello.at[n],
                    inc=1,
                    device_id={"seq": place(v, ring(p, step), q)},
                    device_id_type=MESH,
                )

    def hello_wait(n):
        pl.semaphore_wait(hello.at[n], 4)

    def owner_copy(shard, i):
        target = (ch + i) % WAYS
        return pltpu.make_async_remote_copy(
            src_ref=partial.at[shard, target],
            dst_ref=parts.at[i, shard],
            send_sem=r_send.at[i],
            recv_sem=r_recv.at[i],
            device_id={"ch": target},
            device_id_type=MESH,
        )

    def shard_at(dx, dz):
        return ring(x, dx) * SIDE + ring(z, dz)

    def project(dx, dz):
        shard = shard_at(dx, dz)
        out = mul(wbuf[...], every[shard], NT).astype(BF16).reshape(WAYS, TRIO, CHUNK)
        partial[shard] = out
        parts[0, shard] = partial[shard, ch]
        return shard

    def deliver(shard):
        for i in range(1, WAYS):
            owner_copy(shard, i).start()

    feat_in.wait()
    for v in range(2):
        send(v, "P1+")
        send(v, "P1-")
    for v in range(2):
        send(v, "Q1+0")
        send(v, "Q1-0")
    hello_round(0)

    def param_copy(i):
        return pltpu.make_async_remote_copy(
            src_ref=packed,
            dst_ref=params,
            send_sem=p_send.at[i],
            recv_sem=p_recv,
            device_id={"ch": (ch + i) % WAYS},
            device_id_type=MESH,
        )

    def gain_copy(i):
        return pltpu.make_async_remote_copy(
            src_ref=gain_in,
            dst_ref=gain_got,
            send_sem=k_send.at[i],
            recv_sem=k_recv,
            device_id={"ch": (ch + i) % WAYS},
            device_id_type=MESH,
        )

    for copy in small_in:
        copy.wait()

    @pl.when(at_home)
    def _():
        pltpu.make_async_copy(packed, params, p_recv).start()
        pltpu.make_async_copy(gain_in, gain_got, k_recv).start()
        for i in range(1, WAYS):
            param_copy(i).start()
            gain_copy(i).start()

    def grad_copy(shard, c):
        slot = (shard % 2) * WAYS + c
        return pltpu.make_async_remote_copy(
            src_ref=gbuf.at[slot],
            dst_ref=grads.at[seq],
            send_sem=g_send.at[slot],
            recv_sem=g_recv,
            device_id={"seq": shard, "ch": c},
            device_id_type=MESH,
        )

    def is_self(i):
        return jnp.logical_and(2 * ch + i // WAYS == seq, i % WAYS == ch)

    def give_grads(i, _):
        @pl.when(is_self(i))
        def _():
            pltpu.make_async_copy(gbuf.at[i], grads.at[seq], g_recv).start()

        @pl.when(jnp.logical_not(is_self(i)))
        def _():
            grad_copy(2 * ch + i // WAYS, i % WAYS).start()

        return 0

    weight_in.wait()
    block = count * WAYS
    ordered = None
    for g in range(3):
        pick = chosen(
            (WAYS * TRIO, block),
            lambda r, c: (r % TRIO == 3 * (c % count) + g) & (r // TRIO == c // count),
        )
        part = mul(pick, wraw[g])
        ordered = part if ordered is None else ordered + part
    wbuf[...] = ordered.astype(BF16)
    grads_in.wait()
    pick = chosen(
        (2 * WAYS * ROWS, 2 * block), lambda r, c: (r // ROWS == c // count) & (r % ROWS == c % count)
    )
    gbuf[...] = mul(pick, graw[...]).astype(BF16).reshape(2 * WAYS, ROWS, CHUNK)

    hello_wait(0)
    hello_round(1)
    done = [project(0, 0)]
    hello_wait(1)
    hello_round(2)
    hello_wait(2)
    hello_round(3)

    def follow(dx, dz):
        done.append(project(dx, dz))
        deliver(done[-2])

    prepared = []

    def prepare(number_of):
        for _ in range(number_of):
            if len(prepared) < count:
                tables_of(len(prepared), cols, bands, tables)
                prepared.append(0)

    hello_wait(3)
    lax.fori_loop(0, SHARDS, give_grads, 0)
    arrive(0, "P1+")
    send(0, "P2+")
    send(0, "Q1+1")
    send(0, "Q1-1")
    pltpu.make_async_copy(packed, params, p_recv).wait()
    pltpu.make_async_copy(gain_in, gain_got, k_recv).wait()
    offset = (seq % 2) * block + ch * count
    select_params(count, offset, params, gain_got, cols, rows, gains)
    arrive(0, "P1-")
    send(0, "P2-")
    send(0, "Q1+2")
    send(0, "Q1-2")
    prepare(1)
    arrive(1, "P1+")
    send(1, "P2+")
    send(1, "Q1+1")
    send(1, "Q1-1")
    prepare(1)
    arrive(1, "P1-")
    send(1, "P2-")
    send(1, "Q1+2")
    send(1, "Q1-2")
    prepare(1)
    arrive(0, "Q1+0")
    send(0, "Q2+0")
    follow(0, -1)
    prepare(1)
    arrive(0, "Q1-0")
    send(0, "Q2-0")
    follow(0, 1)
    prepare(1)
    arrive(1, "Q1+0")
    send(1, "Q2+0")
    follow(-1, 0)
    prepare(1)
    arrive(1, "Q1-0")
    send(1, "Q2-0")
    follow(1, 0)
    prepare(1)
    arrive(0, "P2+")
    send(0, "Q1+3a")
    send(0, "Q1-3a")
    prepare(1)
    arrive(0, "P2-")
    send(0, "Q1+3b")
    send(0, "Q1-3b")
    arrive(0, "Q1+1")
    arrive(0, "Q1-1")
    arrive(1, "Q1+1")
    arrive(1, "Q1-1")
    arrive(0, "Q1+2")
    arrive(0, "Q1-2")
    follow(-1, -1)
    follow(1, -1)
    prepare(1)
    arrive(1, "P2+")
    send(1, "Q1+3a")
    send(1, "Q1-3a")
    prepare(1)
    arrive(1, "P2-")
    send(1, "Q1+3b")
    send(1, "Q1-3b")
    send(0, "Q2+1")
    send(0, "Q2-1")
    send(1, "Q2+1")
    send(1, "Q2-1")
    send(0, "Q2+2")
    send(0, "Q2-2")
    prepare(1)
    arrive(1, "Q1+2")
    send(1, "Q2+2")
    follow(-1, 1)
    prepare(1)
    arrive(1, "Q1-2")
    send(1, "Q2-2")
    arrive(1, "Q2+0")
    arrive(1, "Q2-0")
    arrive(0, "Q2+0")
    arrive(0, "Q2-0")
    follow(1, 1)
    follow(2, 0)
    follow(0, 2)
    prepare(1)
    arrive(0, "Q1+3a")
    send(0, "Q2+3")
    arrive(0, "Q1-3a")
    arrive(1, "Q1+3a")
    prepare(1)
    arrive(0, "Q1-3b")
    send(0, "Q2-3")
    send(1, "Q2+3")
    arrive(1, "Q1-3a")
    arrive(0, "Q1+3b")
    prepare(1)
    arrive(1, "Q1-3b")
    send(1, "Q2-3")
    arrive(1, "Q1+3b")
    arrive(0, "Q2+1")
    arrive(0, "Q2-1")
    follow(-1, 2)
    arrive(1, "Q2+1")
    arrive(1, "Q2-1")
    follow(2, -1)
    arrive(0, "Q2+2")
    arrive(0, "Q2-2")
    follow(1, 2)
    arrive(1, "Q2+2")
    arrive(1, "Q2-2")
    follow(2, 1)
    arrive(0, "Q2+3")
    arrive(0, "Q2-3")
    arrive(1, "Q2+3")
    arrive(1, "Q2-3")
    follow(2, 2)
    deliver(done[-1])
    prepare(count)

    pltpu.make_async_copy(gbuf, grads, g_recv).wait()
    for i in range(1, WAYS):
        pltpu.make_async_copy(parts.at[0], parts.at[i], r_recv.at[i]).wait()
    sum_partials(parts, grads, projf, projr, gradf)

    width = SHARDS * CHUNK
    left, right = pl.ds(0, width // 2), pl.ds(width // 2, width // 2)
    whole = pl.ds(0, width)
    tiles = [pl.ds(0, 16), pl.ds(16, 16), pl.ds(32, TRIO - 32)]
    straight = (False, False, True)

    def owner(step, other):
        return ring(y, step) * 2 + (1 - core if other else core)

    def group_copy(t, n, slot, target, lanes, own):
        return pltpu.make_async_remote_copy(
            src_ref=mine.at[tiles[t], lanes] if own else full.at[slot, tiles[t], lanes],
            dst_ref=full.at[slot, tiles[t], lanes],
            send_sem=a_send.at[t, n],
            recv_sem=a_recv.at[t, n],
            device_id={"ch": target},
            device_id_type=MESH,
        )

    relayed = {
        0: (0, 1, False, whole),
        1: (0, -1, False, whole),
        2: (0, 0, True, whole),
        3: (1, 1, False, left),
        4: (-1, -1, False, right),
        5: (1, 0, True, whole),
        6: (-1, 0, True, whole),
        7: (2, 0, True, left),
        8: (2, 0, True, right),
    }
    direct = {n: relayed[n] for n in (0, 1, 2, 5, 6)}
    direct[3] = (0, 2, False, whole)
    direct[7] = (2, 0, True, whole)
    kinds = [direct if straight[t] else relayed for t in range(3)]

    def going(t, n):
        back, step, other, lanes = kinds[t][n]
        return group_copy(t, n, owner(-back, False), owner(step, other), lanes, back == 0)

    def coming(t, n):
        back, step, other, lanes = kinds[t][n]
        return group_copy(t, n, owner(-back - step, other), owner(step, other), lanes, False)

    def own_copy(t):
        return pltpu.make_async_copy(
            mine.at[tiles[t]], full.at[ch, tiles[t]], store_sem.at[t]
        )

    def begin(t):
        for n in (3, 0, 1, 2) if straight[t] else (0, 1, 2):
            going(t, n).start()
        own_copy(t).start()

    def relay(t):
        coming(t, 0).wait_recv()
        if not straight[t]:
            going(t, 3).start()
        going(t, 5).start()
        coming(t, 1).wait_recv()
        if not straight[t]:
            going(t, 4).start()
        going(t, 6).start()

    def relay_far(t):
        coming(t, 3).wait_recv()
        going(t, 7).start()
        if not straight[t]:
            coming(t, 4).wait_recv()
            going(t, 8).start()

    def small_copy(i):
        return pltpu.make_async_remote_copy(
            src_ref=small,
            dst_ref=shared.at[(seq % 2) * WAYS + ch],
            send_sem=s_send.at[i],
            recv_sem=s_recv,
            device_id={"seq": i, "ch": home},
            device_id_type=MESH,
        )

    def small_self(i):
        return jnp.logical_and(i == seq, at_home)

    def start_small(i, _):
        @pl.when(small_self(i))
        def _():
            pltpu.make_async_copy(small, shared.at[(seq % 2) * WAYS + ch], s_recv).start()

        @pl.when(jnp.logical_not(small_self(i)))
        def _():
            small_copy(i).start()

        return 0

    groups = [range(0, 6), range(6, 11), range(11, count)]
    edges = [(0, 16), (16, 32), (32, TRIO)]
    for t in range(3):
        mix_channels(
            groups[t], rows, gains, bands, tables, projf, projr, gradf, small, skips, outs
        )
        pack(outs, mine, *edges[t])
        begin(t)
    finish_small(count, small, skips)
    lax.fori_loop(0, SHARDS, start_small, 0)
    relay(0)
    relay(1)
    relay_far(0)
    relay(2)
    relay_far(1)
    relay_far(2)

    for v in range(2):
        for name, _ in names:
            feature_copy(v, name, False).wait_send()
    for i in range(1, WAYS):
        pltpu.make_async_copy(parts.at[0], parts.at[i], r_send.at[i]).wait()

    def end_sends(i, _):
        @pl.when(jnp.logical_not(is_self(i)))
        def _():
            grad_copy(2 * ch + i // WAYS, i % WAYS).wait_send()

        @pl.when(jnp.logical_not(small_self(i)))
        def _():
            small_copy(i).wait_send()

        return 0

    lax.fori_loop(0, SHARDS, end_sends, 0)

    @pl.when(at_home)
    def _():
        for i in range(1, WAYS):
            param_copy(i).wait_send()
            gain_copy(i).wait_send()

    for t in range(3):
        own_copy(t).wait()
        for n in kinds[t]:
            going(t, n).wait_send()
            if n in (2, 5, 6, 7, 8):
                coming(t, n).wait_recv()
    pltpu.make_async_copy(shared, shared, s_recv).wait()


def finish(
    count, features, full, shared, packed, wgrad, residue_out, rate_out, skip_out, rows
):
    block = count * WAYS
    tokens = full.shape[2]
    width = wgrad.shape[2]
    lanes = pl.ds(pl.multiple_of(pl.program_id(0) * width, width), width)
    right_side = features[:, :, lanes].reshape(tokens, width)
    product = mul(full[...].reshape(WAYS * TRIO, tokens), right_side)
    for part in range(rows.shape[0]):
        lanes = pl.ds(part * CHUNK, CHUNK)
        rows[part] = product[:, part * CHUNK : (part + 1) * CHUNK]
        for owner in range(WAYS):
            for g in range(3):
                own = rows[part, pl.ds(owner * TRIO + g, count, stride=3), :]
                wgrad[g, owner * count : (owner + 1) * count, lanes] = own

    @pl.when(pl.program_id(0) == 0)
    def _():
        pick = chosen(
            (2 * WAYS * ROWS, 2 * block),
            lambda r, c: (r // ROWS == c // count) & (r % ROWS == c % count),
            F32,
        )
        turned = exact(shared[...].reshape(2 * WAYS * ROWS, CHUNK), pick, TN)
        moment = turned[STATE : 2 * STATE] + turned[2 * STATE : 3 * STATE]
        residue_out[...] = turned[0:STATE]
        rate_out[...] = -packed[STATE:] * jnp.exp(packed[0:STATE]) * moment
        skip_out[...] = turned[3 * STATE : 3 * STATE + 1]


def local(features, qkv_weight, grad_out, residues, log_rates, skip_gain):
    width = features.shape[1]
    block = qkv_weight.shape[0]
    count = block // WAYS
    held, order = residues.shape
    weight = qkv_weight.transpose(1, 0, 2)
    anywhere = pl.BlockSpec(memory_space=pl.ANY)
    vmem = pl.BlockSpec(memory_space=pltpu.VMEM)
    dma = pltpu.SemaphoreType.DMA
    tokens = SHARDS * CHUNK
    operands = [
        pltpu.with_memory_space_constraint(array, pltpu.MemorySpace.HBM)
        for array in (
            features, weight, grad_out, log_rates.T, residues.T, skip_gain.reshape(1, held)
        )
    ]
    every, full, shared, packed = pl.pallas_call(
        functools.partial(kernel, count),
        out_shape=(
            jax.ShapeDtypeStruct((SHARDS, CHUNK, width), BF16),
            jax.ShapeDtypeStruct((WAYS, TRIO, tokens), BF16),
            jax.ShapeDtypeStruct((2 * WAYS, ROWS, CHUNK), F32),
            jax.ShapeDtypeStruct((PARAM_ROWS, held), F32),
        ),
        in_specs=[anywhere] * 6,
        out_specs=(vmem,) * 4,
        scratch_shapes=[
            pltpu.VMEM((3, block, width), BF16),
            pltpu.VMEM((WAYS * TRIO, width), BF16),
            pltpu.VMEM((held, CHUNK), BF16),
            pltpu.VMEM((2 * WAYS, ROWS, CHUNK), BF16),
            pltpu.VMEM((SHARDS, WAYS, TRIO, CHUNK), BF16),
            pltpu.VMEM((WAYS, SHARDS, TRIO, CHUNK), BF16),
            pltpu.VMEM((SHARDS, ROWS, CHUNK), BF16),
            pltpu.VMEM((PARAM_ROWS, held), F32),
            pltpu.VMEM((2 * STATE, CHUNK), F32),
            pltpu.VMEM((ROWS, CHUNK), F32),
            pltpu.VMEM((ROWS, CHUNK), F32),
            pltpu.VMEM((ROWS, CHUNK, CHUNK), BF16),
            pltpu.VMEM((ROWS, 11 * STATE, CHUNK), BF16),
            pltpu.VMEM((SHARDS, TRIO, CHUNK), F32),
            pltpu.VMEM((SHARDS, TRIO, CHUNK), F32),
            pltpu.VMEM((SHARDS, ROWS, CHUNK), F32),
            pltpu.VMEM((SHARDS, TRIO, CHUNK), F32),
            pltpu.VMEM((ROWS, CHUNK), F32),
            pltpu.VMEM((ROWS, CHUNK), F32),
            pltpu.VMEM((1, held), F32),
            pltpu.VMEM((1, held), F32),
            pltpu.VMEM((TRIO, tokens), BF16),
            dma((6,)),
            dma((2, 22)),
            dma((2, 22)),
            dma((WAYS,)),
            dma((WAYS,)),
            dma((SHARDS,)),
            dma,
            dma((WAYS,)),
            dma,
            dma((3, 9)),
            dma((3, 9)),
            dma((SHARDS,)),
            dma,
            pltpu.SemaphoreType.REGULAR((4,)),
            dma((WAYS,)),
            dma,
            dma((3,)),
        ],
        compiler_params=pltpu.CompilerParams(
            collective_id=0, has_side_effects=True, vmem_limit_bytes=24 * 2**20
        ),
    )(*operands)
    columns = 512

    def same(*shape):
        return pl.BlockSpec(shape, lambda n: (0,) * len(shape))

    weight_grad, residue_grad, rate_grad, skip_grad = pl.pallas_call(
        functools.partial(finish, count),
        grid=(width // columns,),
        out_shape=(
            jax.ShapeDtypeStruct((3, block, width), F32),
            jax.ShapeDtypeStruct((order, held), F32),
            jax.ShapeDtypeStruct((order, held), F32),
            jax.ShapeDtypeStruct((1, held), F32),
        ),
        in_specs=[
            vmem,
            vmem,
            vmem,
            vmem,
        ],
        out_specs=(
            pl.BlockSpec((3, block, columns), lambda n: (0, 0, n)),
            same(order, held),
            same(order, held),
            same(1, held),
        ),
        scratch_shapes=[pltpu.VMEM((columns // CHUNK, WAYS * TRIO, CHUNK), F32)],
        compiler_params=pltpu.CompilerParams(vmem_limit_bytes=24 * 2**20),
    )(every, full, shared, packed)
    return weight_grad.transpose(1, 0, 2), residue_grad.T, rate_grad.T, skip_grad.reshape(held)


def solution(mesh):
    placed = (
        P("seq", "ch"),
        P("seq", None, "ch"),
        P("ch", "seq"),
        P("ch", None),
        P("ch", None),
        P("ch"),
    )
    return jax.shard_map(
        local,
        mesh=mesh,
        in_specs=placed,
        out_specs=(P("seq", None, "ch"), P("ch", None), P("ch", None), P("ch")),
        check_vma=False,
    )
```

```python
import functools

import jax
import jax.numpy as jnp
from jax import lax
from jax.experimental import pallas as pl
from jax.experimental.pallas import tpu as pltpu
from jax.sharding import PartitionSpec as P

F32, BF16 = jnp.float32, jnp.bfloat16
CHUNK = 128
SIDE = 4
SHARDS = SIDE * SIDE
WAYS = 2 * SIDE
ROWS = 16
TRIO = 40
STATE = 16
LATE = 5
MESH = pl.DeviceIdType.MESH
PARAM_ROWS = 2 * STATE

NT = (((1,), (1,)), ((), ()))
TN = (((0,), (0,)), ((), ()))
NN = (((1,), (0,)), ((), ()))


def mul(a, b, dims=NN):
    return lax.dot_general(a, b, dims, preferred_element_type=F32)


def exact(a, b, dims=NN):
    return lax.dot_general(a, b, dims, precision="highest", preferred_element_type=F32)


def iota(shape, dim):
    return lax.broadcasted_iota(jnp.int32, shape, dim)


def chosen(shape, rule, kind=BF16):
    return rule(iota(shape, 0), iota(shape, 1)).astype(kind)


def sum_partials(shards, parts, grads, projf, projr, gradf):
    flip = chosen((CHUNK, CHUNK), lambda r, c: r + c == CHUNK - 1)
    for k in shards:
        total = parts[0, k].astype(F32)
        for way in range(1, WAYS):
            total = total + parts[way, k].astype(F32)
        rounded = total.astype(BF16)
        projf[k] = rounded.astype(F32)
        projr[k] = mul(rounded, flip)
        gradf[k] = grads[k].astype(F32)


def carry(values, step, lagged, reverse):
    row = iota(values.shape, 0)
    shape = values.shape
    decay = jnp.broadcast_to(step, shape)
    reach = 1
    while reach < shape[0]:
        amount = shape[0] - reach if reverse else reach
        keep = row < shape[0] - reach if reverse else row >= reach
        near = jnp.where(keep, decay * pltpu.roll(values, amount, 0), 0.0)
        if lagged is not None:
            moved = jnp.where(keep, decay * pltpu.roll(lagged, amount, 0), 0.0)
            lagged = lagged + moved + (CHUNK * reach) * near
        values = values + near
        decay = decay * decay
        reach *= 2
    return values, lagged


def before(values, reverse):
    row = iota(values.shape, 0)
    last = values.shape[0] - 1
    if reverse:
        return jnp.where(row < last, pltpu.roll(values, last, 0), 0.0)
    return jnp.where(row >= 1, pltpu.roll(values, 1, 0), 0.0)


def select_params(count, offset, params, gain, cols, rows, gains):
    lanes = params.shape[1]
    down = chosen((lanes, CHUNK), lambda r, c: (r == c + offset) & (c < count), F32)
    across = chosen((ROWS, lanes), lambda r, c: (c == r + offset) & (r < count), F32)
    cols[...] = exact(params[0 : 2 * STATE], down)
    rates = params[0:STATE]
    rows[:, 0 : 3 * STATE] = exact(across, jnp.concatenate([rates, rates, rates], 0), NT)
    gains[...] = exact(across, jnp.broadcast_to(gain[...], (CHUNK, lanes)), NT)


def tables_of(c, cols, bands, tables):
    lane = iota((STATE, CHUNK), 1).astype(F32)
    rates = jnp.exp(cols[0:STATE, c : c + 1])
    residues = cols[STATE : 2 * STATE, c : c + 1]
    near = jnp.exp(-rates * lane)
    far = jnp.exp(-rates * (CHUNK - lane))
    weighted = residues * near
    taps = jnp.sum(weighted, axis=0, keepdims=True)
    upper = iota((CHUNK, CHUNK), 1) >= iota((CHUNK, CHUNK), 0)
    spread = pltpu.roll(jnp.broadcast_to(taps, (CHUNK, CHUNK)), 0, 1, stride=1, stride_axis=0)
    bands[c] = jnp.where(upper, spread, 0.0).astype(BF16)
    far_lag = (far * (CHUNK - lane)).astype(BF16)
    blocks = [near, near * lane, near, far, far, far, None, None, None, weighted, residues * far]
    for at, block in enumerate(blocks):
        tables[c, at * STATE : (at + 1) * STATE] = far_lag if block is None else block.astype(BF16)


def mix_channels(group, rows, gains, bands, tables, projf, projr, gradf, small, skips, outs):
    lower = iota((CHUNK, CHUNK), 1) <= iota((CHUNK, CHUNK), 0)
    third = iota((SHARDS, 3 * STATE), 1) < 2 * STATE
    kvs, gms, firsts = {}, {}, {}
    for c in group:
        kv = projf[:, 3 * c + 1, :] * projf[:, 3 * c + 2, :]
        gm = gradf[:, c, :] * projf[:, 3 * c, :]
        back = projr[:, 3 * c + 1, :] * projr[:, 3 * c + 2, :]
        kvs[c], gms[c] = kv, gm
        skips[c : c + 1] = jnp.sum(kv * gm, axis=0, keepdims=True)
        kv, gm, back = kv.astype(BF16), gm.astype(BF16), back.astype(BF16)
        firsts[c] = (
            mul(kv, tables[c, 3 * STATE : 6 * STATE], NT),
            mul(kv, tables[c, 6 * STATE : 9 * STATE], NT),
            mul(gm, tables[c, 0 : 3 * STATE], NT),
            mul(back, gm, TN),
            mul(kv, bands[c]),
            mul(gm, bands[c], NT),
        )
    seconds = {}
    for c in group:
        tails, tails_lag, heads, product, _, _ = firsts[c]
        step = jnp.exp(-CHUNK * jnp.exp(rows[c : c + 1, 0 : 3 * STATE]))
        states, states_lag = carry(tails, step, tails_lag, False)
        states, states_lag = before(states, False), before(states_lag, False)
        inter = jnp.sum(heads * jnp.where(third, states, states_lag), axis=0, keepdims=True)
        adjoints, _ = carry(heads[:, 0:STATE], step[:, 0:STATE], None, True)
        adjoints = before(adjoints, True)
        skewed = pltpu.roll(product, 1, 1, stride=1, stride_axis=0)
        sums = jnp.sum(jnp.where(lower, skewed, 0.0), axis=0, keepdims=True)
        wide = jnp.broadcast_to(sums, (ROWS, CHUNK)).astype(BF16)
        seconds[c] = (
            mul(states[:, 0:STATE].astype(BF16), tables[c, 9 * STATE : 10 * STATE]),
            mul(adjoints.astype(BF16), tables[c, 10 * STATE : 11 * STATE]),
            mul(wide, tables[c, 0 : 2 * STATE], NT),
            inter,
        )
    for c in group:
        conv, corr, intra, inter = seconds[c]
        gain = gains[c : c + 1]
        conv = conv + firsts[c][4] + gain * kvs[c]
        grad_mix = corr + firsts[c][5] + gain * gms[c]
        outs[:, 3 * c, :] = gradf[:, c, :] * conv
        outs[:, 3 * c + 1, :] = grad_mix * projf[:, 3 * c + 2, :]
        outs[:, 3 * c + 2, :] = grad_mix * projf[:, 3 * c + 1, :]
        small[c : c + 1, 0 : 3 * STATE] = inter
        small[c : c + 1, 0 : 2 * STATE] += intra[0:1]


def pack(outs, mine, first, last):
    for k in range(SHARDS):
        mine[first:last, k * CHUNK : (k + 1) * CHUNK] = outs[k, first:last].astype(BF16)


def finish_small(count, small, skips, tight):
    lane = iota((ROWS, CHUNK), 1)
    row = iota((ROWS, CHUNK), 0)
    summed = jnp.sum(skips[...], axis=1, keepdims=True)
    filled = jnp.where(lane == 3 * STATE, summed, small[...])
    filled = jnp.where(row < count, filled, 0.0)
    half = ROWS // 2
    upper = pltpu.roll(filled[half:], CHUNK // 2, 1)
    tight[...] = jnp.where(lane[:half] < CHUNK // 2, filled[:half], upper)


def kernel(
    count, feat, weight, gout, rates_t, residues_t, gain, every, full, shared, packed,
    wraw, wbuf, graw, gbuf, partial, parts, grads, params, cols, rows, gains, bands,
    tables, projf, projr, gradf, outs, small, skips, gain_in, gain_got, mine, tight,
    local_sem, f_send, f_recv, r_send, r_recv, g_send, g_recv, p_send, p_recv, a_send, a_recv,
    s_send, s_recv, hello, k_send, k_recv, store_sem,
):
    seq, ch = lax.axis_index("seq"), lax.axis_index("ch")
    x, z = seq // SIDE, seq % SIDE
    y, core = ch // 2, ch % 2
    home = seq // 2
    at_home = ch == home

    feat_in = pltpu.make_async_copy(feat, every.at[seq], local_sem.at[0])
    weight_in = pltpu.make_async_copy(weight, wraw, local_sem.at[1])
    grads_in = pltpu.make_async_copy(gout, graw, local_sem.at[2])
    small_in = [
        pltpu.make_async_copy(rates_t, packed.at[pl.ds(0, STATE)], local_sem.at[3]),
        pltpu.make_async_copy(residues_t, packed.at[pl.ds(STATE, STATE)], local_sem.at[4]),
        pltpu.make_async_copy(gain, gain_in, local_sem.at[5]),
    ]
    feat_in.start()
    for copy in small_in:
        copy.start()
    weight_in.start()
    grads_in.start()

    def ring(value, step):
        return (value + step + SIDE) % SIDE

    def place(v, p, q):
        return p * SIDE + q if v == 0 else q * SIDE + p

    def spot(v):
        return (x, z) if v == 0 else (z, x)

    barrier = pltpu.get_barrier_semaphore()

    def greet(s, c):
        pl.semaphore_signal(barrier, inc=1, device_id={"seq": s, "ch": c}, device_id_type=MESH)

    for v in range(2):
        p, q = spot(v)
        for step in (-1, 1):
            greet(place(v, ring(p, step), q), ch)
    for i in range(1, WAYS):
        greet(seq, (ch + i) % WAYS)
    small[...] = jnp.zeros_like(small)
    skips[...] = jnp.zeros_like(skips)
    outs[:, TRIO - 1, :] = jnp.zeros((SHARDS, CHUNK), F32)
    pl.semaphore_wait(barrier, 4 + WAYS - 1)

    half, quarter = CHUNK // 2, CHUNK // 4
    offs = (0, -1, 1, 2)

    def piece(v, part):
        start = v * half + (quarter if part == "b" else 0)
        return pl.ds(start, half if part == "h" else quarter)

    names = [("P1+", "h"), ("P1-", "h"), ("P2+", "a"), ("P2-", "b")]
    for j in range(3):
        names += [(f"Q1+{j}", "h"), (f"Q1-{j}", "h"), (f"Q2+{j}", "a"), (f"Q2-{j}", "b")]
    names += [("Q1+3a", "a"), ("Q1+3b", "b"), ("Q1-3a", "a"), ("Q1-3b", "b")]
    names += [("Q2+3", "a"), ("Q2-3", "b")]
    number = {name: n for n, (name, _) in enumerate(names)}
    piece_of = dict(names)

    def feature_copy(v, name, arriving):
        p, q = spot(v)
        step = 1 if name[2] == "+" else -1
        hops = int(name[1]) - 1 + (1 if arriving else 0)
        if name[0] == "P":
            source = place(v, ring(p, -step * hops), q)
            target = place(v, ring(p, step), q)
        else:
            source = place(v, ring(p, offs[int(name[3])]), ring(q, -step * hops))
            target = place(v, p, ring(q, step))
        rows = piece(v, piece_of[name])
        return pltpu.make_async_remote_copy(
            src_ref=every.at[source, rows],
            dst_ref=every.at[source, rows],
            send_sem=f_send.at[v, number[name]],
            recv_sem=f_recv.at[v, number[name]],
            device_id={"seq": target},
            device_id_type=MESH,
        )

    def send(v, name):
        feature_copy(v, name, False).start()

    def arrive(v, name):
        feature_copy(v, name, True).wait_recv()

    def hello_round(n):
        for v in range(2):
            p, q = spot(v)
            for step in (-1, 1):
                pl.semaphore_signal(
                    hello.at[n],
                    inc=1,
                    device_id={"seq": place(v, ring(p, step), q)},
                    device_id_type=MESH,
                )

    def hello_wait(n):
        pl.semaphore_wait(hello.at[n], 4)

    def owner_copy(shard, i, batch):
        target = (ch + i) % WAYS
        return pltpu.make_async_remote_copy(
            src_ref=partial.at[shard, target],
            dst_ref=parts.at[i, shard],
            send_sem=r_send.at[batch, i],
            recv_sem=r_recv.at[batch, i],
            device_id={"ch": target},
            device_id_type=MESH,
        )

    def shard_at(dx, dz):
        return ring(x, dx) * SIDE + ring(z, dz)

    def project(dx, dz):
        shard = shard_at(dx, dz)
        out = mul(wbuf[...], every[shard], NT).astype(BF16).reshape(WAYS, TRIO, CHUNK)
        partial[shard] = out
        parts[0, shard] = partial[shard, ch]
        return shard

    def deliver(at):
        for i in range(1, WAYS):
            owner_copy(done[at], i, 0 if at < SHARDS - LATE else 1).start()

    def await_batch(batch, sems):
        size = LATE if batch else SHARDS - LATE
        for i in range(1, WAYS):
            block_of = parts.at[i, pl.ds(0, size)]
            pltpu.make_async_copy(block_of, block_of, sems.at[batch, i]).wait()

    feat_in.wait()
    for v in range(2):
        send(v, "P1+")
        send(v, "P1-")
    for v in range(2):
        send(v, "Q1+0")
        send(v, "Q1-0")
    hello_round(0)

    def param_copy(i):
        return pltpu.make_async_remote_copy(
            src_ref=packed,
            dst_ref=params,
            send_sem=p_send.at[i],
            recv_sem=p_recv,
            device_id={"ch": (ch + i) % WAYS},
            device_id_type=MESH,
        )

    def gain_copy(i):
        return pltpu.make_async_remote_copy(
            src_ref=gain_in,
            dst_ref=gain_got,
            send_sem=k_send.at[i],
            recv_sem=k_recv,
            device_id={"ch": (ch + i) % WAYS},
            device_id_type=MESH,
        )

    for copy in small_in:
        copy.wait()

    @pl.when(at_home)
    def _():
        pltpu.make_async_copy(packed, params, p_recv).start()
        pltpu.make_async_copy(gain_in, gain_got, k_recv).start()
        for i in range(1, WAYS):
            param_copy(i).start()
            gain_copy(i).start()

    def grad_copy(shard, c):
        slot = (shard % 2) * WAYS + c
        return pltpu.make_async_remote_copy(
            src_ref=gbuf.at[slot],
            dst_ref=grads.at[seq],
            send_sem=g_send.at[slot],
            recv_sem=g_recv,
            device_id={"seq": shard, "ch": c},
            device_id_type=MESH,
        )

    def is_self(i):
        return jnp.logical_and(2 * ch + i // WAYS == seq, i % WAYS == ch)

    def give_grads(i, _):
        @pl.when(is_self(i))
        def _():
            pltpu.make_async_copy(gbuf.at[i], grads.at[seq], g_recv).start()

        @pl.when(jnp.logical_not(is_self(i)))
        def _():
            grad_copy(2 * ch + i // WAYS, i % WAYS).start()

        return 0

    weight_in.wait()
    block = count * WAYS
    ordered = None
    for g in range(3):
        pick = chosen(
            (WAYS * TRIO, block),
            lambda r, c: (r % TRIO == 3 * (c % count) + g) & (r // TRIO == c // count),
        )
        part = mul(pick, wraw[g])
        ordered = part if ordered is None else ordered + part
    wbuf[...] = ordered.astype(BF16)
    grads_in.wait()
    pick = chosen(
        (2 * WAYS * ROWS, 2 * block), lambda r, c: (r // ROWS == c // count) & (r % ROWS == c % count)
    )
    gbuf[...] = mul(pick, graw[...]).astype(BF16).reshape(2 * WAYS, ROWS, CHUNK)

    hello_wait(0)
    hello_round(1)
    done = [project(0, 0)]
    hello_wait(1)
    hello_round(2)
    hello_wait(2)
    hello_round(3)

    def follow(dx, dz):
        done.append(project(dx, dz))
        deliver(len(done) - 2)

    prepared = []

    def prepare(number_of):
        for _ in range(number_of):
            if len(prepared) < count:
                tables_of(len(prepared), cols, bands, tables)
                prepared.append(0)

    hello_wait(3)
    arrive(0, "P1+")
    send(0, "P2+")
    send(0, "Q1+1")
    send(0, "Q1-1")
    pltpu.make_async_copy(packed, params, p_recv).wait()
    pltpu.make_async_copy(gain_in, gain_got, k_recv).wait()
    offset = (seq % 2) * block + ch * count
    select_params(count, offset, params, gain_got, cols, rows, gains)
    arrive(0, "P1-")
    send(0, "P2-")
    send(0, "Q1+2")
    send(0, "Q1-2")
    prepare(1)
    arrive(1, "P1+")
    send(1, "P2+")
    send(1, "Q1+1")
    send(1, "Q1-1")
    prepare(1)
    arrive(1, "P1-")
    send(1, "P2-")
    send(1, "Q1+2")
    send(1, "Q1-2")
    prepare(1)
    arrive(0, "Q1+0")
    send(0, "Q2+0")
    follow(0, -1)
    prepare(1)
    arrive(0, "Q1-0")
    send(0, "Q2-0")
    follow(0, 1)
    prepare(1)
    arrive(1, "Q1+0")
    send(1, "Q2+0")
    follow(-1, 0)
    prepare(1)
    arrive(1, "Q1-0")
    send(1, "Q2-0")
    follow(1, 0)
    prepare(1)
    arrive(0, "P2+")
    send(0, "Q1+3a")
    send(0, "Q1-3a")
    prepare(1)
    arrive(0, "P2-")
    send(0, "Q1+3b")
    send(0, "Q1-3b")
    arrive(0, "Q1+1")
    arrive(0, "Q1-1")
    arrive(1, "Q1+1")
    arrive(1, "Q1-1")
    arrive(0, "Q1+2")
    arrive(0, "Q1-2")
    follow(-1, -1)
    follow(1, -1)
    prepare(1)
    arrive(1, "P2+")
    send(1, "Q1+3a")
    send(1, "Q1-3a")
    prepare(1)
    arrive(1, "P2-")
    send(1, "Q1+3b")
    send(1, "Q1-3b")
    send(0, "Q2+1")
    send(0, "Q2-1")
    send(1, "Q2+1")
    send(1, "Q2-1")
    send(0, "Q2+2")
    send(0, "Q2-2")
    prepare(1)
    arrive(1, "Q1+2")
    send(1, "Q2+2")
    follow(-1, 1)
    prepare(1)
    arrive(1, "Q1-2")
    send(1, "Q2-2")
    arrive(1, "Q2+0")
    arrive(1, "Q2-0")
    arrive(0, "Q2+0")
    arrive(0, "Q2-0")
    follow(1, 1)
    follow(2, 0)
    follow(0, 2)
    prepare(1)
    arrive(0, "Q1+3a")
    send(0, "Q2+3")
    arrive(0, "Q1-3a")
    arrive(1, "Q1+3a")
    prepare(1)
    arrive(0, "Q1-3b")
    send(0, "Q2-3")
    send(1, "Q2+3")
    arrive(1, "Q1-3a")
    arrive(0, "Q1+3b")
    prepare(1)
    arrive(1, "Q1-3b")
    send(1, "Q2-3")
    lax.fori_loop(0, SHARDS, give_grads, 0)
    arrive(1, "Q1+3b")
    arrive(0, "Q2+1")
    arrive(0, "Q2-1")
    follow(-1, 2)
    arrive(1, "Q2+1")
    arrive(1, "Q2-1")
    follow(2, -1)
    arrive(0, "Q2+2")
    arrive(0, "Q2-2")
    follow(1, 2)
    arrive(1, "Q2+2")
    arrive(1, "Q2-2")
    follow(2, 1)
    arrive(0, "Q2+3")
    arrive(0, "Q2-3")
    arrive(1, "Q2+3")
    arrive(1, "Q2-3")
    follow(2, 2)
    deliver(SHARDS - 1)
    prepare(count)

    pltpu.make_async_copy(gbuf, grads, g_recv).wait()
    await_batch(0, r_recv)
    sum_partials(done[: SHARDS - LATE], parts, grads, projf, projr, gradf)
    await_batch(1, r_recv)
    sum_partials(done[SHARDS - LATE :], parts, grads, projf, projr, gradf)

    width = SHARDS * CHUNK
    left, right = pl.ds(0, width // 2), pl.ds(width // 2, width // 2)
    whole = pl.ds(0, width)
    tiles = [pl.ds(0, 16), pl.ds(16, 16), pl.ds(32, TRIO - 32)]
    straight = (False, False, True)

    def owner(step, other):
        return ring(y, step) * 2 + (1 - core if other else core)

    def group_copy(t, n, slot, target, lanes, own):
        return pltpu.make_async_remote_copy(
            src_ref=mine.at[tiles[t], lanes] if own else full.at[slot, tiles[t], lanes],
            dst_ref=full.at[slot, tiles[t], lanes],
            send_sem=a_send.at[t, n],
            recv_sem=a_recv.at[t, n],
            device_id={"ch": target},
            device_id_type=MESH,
        )

    relayed = {
        0: (0, 1, False, whole),
        1: (0, -1, False, whole),
        2: (0, 0, True, whole),
        3: (1, 1, False, left),
        4: (-1, -1, False, right),
        5: (1, 0, True, whole),
        6: (-1, 0, True, whole),
        7: (2, 0, True, left),
        8: (2, 0, True, right),
    }
    direct = {n: relayed[n] for n in (0, 1, 2, 5, 6)}
    direct[3] = (0, 2, False, whole)
    direct[7] = (2, 0, True, whole)
    kinds = [direct if straight[t] else relayed for t in range(3)]

    def going(t, n):
        back, step, other, lanes = kinds[t][n]
        return group_copy(t, n, owner(-back, False), owner(step, other), lanes, back == 0)

    def coming(t, n):
        back, step, other, lanes = kinds[t][n]
        return group_copy(t, n, owner(-back - step, other), owner(step, other), lanes, False)

    def own_copy(t):
        return pltpu.make_async_copy(
            mine.at[tiles[t]], full.at[ch, tiles[t]], store_sem.at[t]
        )

    def begin(t):
        for n in (3, 0, 1, 2) if straight[t] else (0, 1, 2):
            going(t, n).start()
        own_copy(t).start()

    def relay(t):
        coming(t, 0).wait_recv()
        if not straight[t]:
            going(t, 3).start()
        going(t, 5).start()
        coming(t, 1).wait_recv()
        if not straight[t]:
            going(t, 4).start()
        going(t, 6).start()

    def relay_far(t):
        coming(t, 3).wait_recv()
        going(t, 7).start()
        if not straight[t]:
            coming(t, 4).wait_recv()
            going(t, 8).start()

    def small_copy(i):
        return pltpu.make_async_remote_copy(
            src_ref=tight,
            dst_ref=shared.at[(seq % 2) * WAYS + ch],
            send_sem=s_send.at[i],
            recv_sem=s_recv,
            device_id={"seq": i, "ch": home},
            device_id_type=MESH,
        )

    def small_self(i):
        return jnp.logical_and(i == seq, at_home)

    def start_small(i, _):
        @pl.when(small_self(i))
        def _():
            pltpu.make_async_copy(tight, shared.at[(seq % 2) * WAYS + ch], s_recv).start()

        @pl.when(jnp.logical_not(small_self(i)))
        def _():
            small_copy(i).start()

        return 0

    groups = [range(0, 6), range(6, 11), range(11, count)]
    edges = [(0, 16), (16, 32), (32, TRIO)]
    for t in range(3):
        mix_channels(
            groups[t], rows, gains, bands, tables, projf, projr, gradf, small, skips, outs
        )
        pack(outs, mine, *edges[t])
        begin(t)
    finish_small(count, small, skips, tight)
    relay(0)
    lax.fori_loop(0, SHARDS, start_small, 0)
    relay(1)
    relay_far(0)
    relay(2)
    relay_far(1)
    relay_far(2)

    for v in range(2):
        for name, _ in names:
            feature_copy(v, name, False).wait_send()
    await_batch(0, r_send)
    await_batch(1, r_send)

    def end_sends(i, _):
        @pl.when(jnp.logical_not(is_self(i)))
        def _():
            grad_copy(2 * ch + i // WAYS, i % WAYS).wait_send()

        @pl.when(jnp.logical_not(small_self(i)))
        def _():
            small_copy(i).wait_send()

        return 0

    lax.fori_loop(0, SHARDS, end_sends, 0)

    @pl.when(at_home)
    def _():
        for i in range(1, WAYS):
            param_copy(i).wait_send()
            gain_copy(i).wait_send()

    for t in range(3):
        own_copy(t).wait()
        for n in kinds[t]:
            going(t, n).wait_send()
            if n in (2, 5, 6, 7, 8):
                coming(t, n).wait_recv()
    pltpu.make_async_copy(shared, shared, s_recv).wait()


def finish(
    count, features, full, shared, packed, wgrad, residue_out, rate_out, skip_out, rows
):
    block = count * WAYS
    tokens = full.shape[2]
    width = wgrad.shape[2]
    lanes = pl.ds(pl.multiple_of(pl.program_id(0) * width, width), width)
    right_side = features[:, :, lanes].reshape(tokens, width)
    product = mul(full[...].reshape(WAYS * TRIO, tokens), right_side)
    for part in range(rows.shape[0]):
        lanes = pl.ds(part * CHUNK, CHUNK)
        rows[part] = product[:, part * CHUNK : (part + 1) * CHUNK]
        for owner in range(WAYS):
            for g in range(3):
                own = rows[part, pl.ds(owner * TRIO + g, count, stride=3), :]
                wgrad[g, owner * count : (owner + 1) * count, lanes] = own

    @pl.when(pl.program_id(0) == 0)
    def _():
        half = ROWS // 2
        tiles = shared[...].reshape(2 * WAYS * half, CHUNK)
        turned = []
        for first in (0, half):
            pick = chosen(
                (2 * WAYS * half, 2 * block),
                lambda r, c: (r // half == c // count) & (r % half + first == c % count),
                F32,
            )
            turned.append(exact(tiles, pick, TN))
        turned = turned[0][: CHUNK // 2] + turned[1][CHUNK // 2 :]
        moment = turned[STATE : 2 * STATE] + turned[2 * STATE : 3 * STATE]
        residue_out[...] = turned[0:STATE]
        rate_out[...] = -packed[STATE:] * jnp.exp(packed[0:STATE]) * moment
        skip_out[...] = turned[3 * STATE : 3 * STATE + 1]


def local(features, qkv_weight, grad_out, residues, log_rates, skip_gain):
    width = features.shape[1]
    block = qkv_weight.shape[0]
    count = block // WAYS
    held, order = residues.shape
    weight = qkv_weight.transpose(1, 0, 2)
    anywhere = pl.BlockSpec(memory_space=pl.ANY)
    vmem = pl.BlockSpec(memory_space=pltpu.VMEM)
    dma = pltpu.SemaphoreType.DMA
    tokens = SHARDS * CHUNK
    operands = [
        pltpu.with_memory_space_constraint(array, pltpu.MemorySpace.HBM)
        for array in (
            features, weight, grad_out, log_rates.T, residues.T, skip_gain.reshape(1, held)
        )
    ]
    every, full, shared, packed = pl.pallas_call(
        functools.partial(kernel, count),
        out_shape=(
            jax.ShapeDtypeStruct((SHARDS, CHUNK, width), BF16),
            jax.ShapeDtypeStruct((WAYS, TRIO, tokens), BF16),
            jax.ShapeDtypeStruct((2 * WAYS, ROWS // 2, CHUNK), F32),
            jax.ShapeDtypeStruct((PARAM_ROWS, held), F32),
        ),
        in_specs=[anywhere] * 6,
        out_specs=(vmem,) * 4,
        scratch_shapes=[
            pltpu.VMEM((3, block, width), BF16),
            pltpu.VMEM((WAYS * TRIO, width), BF16),
            pltpu.VMEM((held, CHUNK), BF16),
            pltpu.VMEM((2 * WAYS, ROWS, CHUNK), BF16),
            pltpu.VMEM((SHARDS, WAYS, TRIO, CHUNK), BF16),
            pltpu.VMEM((WAYS, SHARDS, TRIO, CHUNK), BF16),
            pltpu.VMEM((SHARDS, ROWS, CHUNK), BF16),
            pltpu.VMEM((PARAM_ROWS, held), F32),
            pltpu.VMEM((2 * STATE, CHUNK), F32),
            pltpu.VMEM((ROWS, CHUNK), F32),
            pltpu.VMEM((ROWS, CHUNK), F32),
            pltpu.VMEM((ROWS, CHUNK, CHUNK), BF16),
            pltpu.VMEM((ROWS, 11 * STATE, CHUNK), BF16),
            pltpu.VMEM((SHARDS, TRIO, CHUNK), F32),
            pltpu.VMEM((SHARDS, TRIO, CHUNK), F32),
            pltpu.VMEM((SHARDS, ROWS, CHUNK), F32),
            pltpu.VMEM((SHARDS, TRIO, CHUNK), F32),
            pltpu.VMEM((ROWS, CHUNK), F32),
            pltpu.VMEM((ROWS, CHUNK), F32),
            pltpu.VMEM((1, held), F32),
            pltpu.VMEM((1, held), F32),
            pltpu.VMEM((TRIO, tokens), BF16),
            pltpu.VMEM((ROWS // 2, CHUNK), F32),
            dma((6,)),
            dma((2, 22)),
            dma((2, 22)),
            dma((2, WAYS)),
            dma((2, WAYS)),
            dma((SHARDS,)),
            dma,
            dma((WAYS,)),
            dma,
            dma((3, 9)),
            dma((3, 9)),
            dma((SHARDS,)),
            dma,
            pltpu.SemaphoreType.REGULAR((4,)),
            dma((WAYS,)),
            dma,
            dma((3,)),
        ],
        compiler_params=pltpu.CompilerParams(
            collective_id=0, has_side_effects=True, vmem_limit_bytes=24 * 2**20
        ),
    )(*operands)
    columns = 512

    def same(*shape):
        return pl.BlockSpec(shape, lambda n: (0,) * len(shape))

    weight_grad, residue_grad, rate_grad, skip_grad = pl.pallas_call(
        functools.partial(finish, count),
        grid=(width // columns,),
        out_shape=(
            jax.ShapeDtypeStruct((3, block, width), F32),
            jax.ShapeDtypeStruct((order, held), F32),
            jax.ShapeDtypeStruct((order, held), F32),
            jax.ShapeDtypeStruct((1, held), F32),
        ),
        in_specs=[
            vmem,
            vmem,
            vmem,
            vmem,
        ],
        out_specs=(
            pl.BlockSpec((3, block, columns), lambda n: (0, 0, n)),
            same(order, held),
            same(order, held),
            same(1, held),
        ),
        scratch_shapes=[pltpu.VMEM((columns // CHUNK, WAYS * TRIO, CHUNK), F32)],
        compiler_params=pltpu.CompilerParams(vmem_limit_bytes=24 * 2**20),
    )(every, full, shared, packed)
    return weight_grad.transpose(1, 0, 2), residue_grad.T, rate_grad.T, skip_grad.reshape(held)


def solution(mesh):
    placed = (
        P("seq", "ch"),
        P("seq", None, "ch"),
        P("ch", "seq"),
        P("ch", None),
        P("ch", None),
        P("ch"),
    )
    return jax.shard_map(
        local,
        mesh=mesh,
        in_specs=placed,
        out_specs=(P("seq", None, "ch"), P("ch", None), P("ch", None), P("ch")),
        check_vma=False,
    )
```

```python
import functools

import jax
import jax.numpy as jnp
from jax import lax
from jax.experimental import pallas as pl
from jax.experimental.pallas import tpu as pltpu
from jax.sharding import PartitionSpec as P

F32, BF16 = jnp.float32, jnp.bfloat16
CHUNK = 128
SIDE = 4
SHARDS = SIDE * SIDE
WAYS = 2 * SIDE
ROWS = 16
TRIO = 40
STATE = 16
LATE = 5
MESH = pl.DeviceIdType.MESH
PARAM_ROWS = 2 * STATE

NT = (((1,), (1,)), ((), ()))
TN = (((0,), (0,)), ((), ()))
NN = (((1,), (0,)), ((), ()))


def mul(a, b, dims=NN):
    return lax.dot_general(a, b, dims, preferred_element_type=F32)


def exact(a, b, dims=NN):
    return lax.dot_general(a, b, dims, precision="highest", preferred_element_type=F32)


def iota(shape, dim):
    return lax.broadcasted_iota(jnp.int32, shape, dim)


def chosen(shape, rule, kind=BF16):
    return rule(iota(shape, 0), iota(shape, 1)).astype(kind)


def sum_partials(shards, parts, grads, projf, projr, gradf):
    flip = chosen((CHUNK, CHUNK), lambda r, c: r + c == CHUNK - 1)
    for k in shards:
        total = parts[0, k].astype(F32)
        for way in range(1, WAYS):
            total = total + parts[way, k].astype(F32)
        rounded = total.astype(BF16)
        projf[k] = rounded.astype(F32)
        projr[k] = mul(rounded, flip)
        gradf[k] = grads[k].astype(F32)


def carry(values, step, lagged, reverse):
    row = iota(values.shape, 0)
    shape = values.shape
    decay = jnp.broadcast_to(step, shape)
    reach = 1
    while reach < shape[0]:
        amount = shape[0] - reach if reverse else reach
        keep = row < shape[0] - reach if reverse else row >= reach
        near = jnp.where(keep, decay * pltpu.roll(values, amount, 0), 0.0)
        if lagged is not None:
            moved = jnp.where(keep, decay * pltpu.roll(lagged, amount, 0), 0.0)
            lagged = lagged + moved + (CHUNK * reach) * near
        values = values + near
        decay = decay * decay
        reach *= 2
    return values, lagged


def before(values, reverse):
    row = iota(values.shape, 0)
    last = values.shape[0] - 1
    if reverse:
        return jnp.where(row < last, pltpu.roll(values, last, 0), 0.0)
    return jnp.where(row >= 1, pltpu.roll(values, 1, 0), 0.0)


def select_params(count, offset, params, gain, cols, rows, gains):
    lanes = params.shape[1]
    down = chosen((lanes, CHUNK), lambda r, c: (r == c + offset) & (c < count), F32)
    across = chosen((ROWS, lanes), lambda r, c: (c == r + offset) & (r < count), F32)
    cols[...] = exact(params[0 : 2 * STATE], down)
    rates = params[0:STATE]
    rows[:, 0 : 3 * STATE] = exact(across, jnp.concatenate([rates, rates, rates], 0), NT)
    gains[...] = exact(across, jnp.broadcast_to(gain[...], (CHUNK, lanes)), NT)


def tables_of(c, cols, bands, tables):
    lane = iota((STATE, CHUNK), 1).astype(F32)
    rates = jnp.exp(cols[0:STATE, c : c + 1])
    residues = cols[STATE : 2 * STATE, c : c + 1]
    near = jnp.exp(-rates * lane)
    far = jnp.exp(-rates * (CHUNK - lane))
    weighted = residues * near
    taps = jnp.sum(weighted, axis=0, keepdims=True)
    upper = iota((CHUNK, CHUNK), 1) >= iota((CHUNK, CHUNK), 0)
    spread = pltpu.roll(jnp.broadcast_to(taps, (CHUNK, CHUNK)), 0, 1, stride=1, stride_axis=0)
    bands[c] = jnp.where(upper, spread, 0.0).astype(BF16)
    far_lag = (far * (CHUNK - lane)).astype(BF16)
    blocks = [near, near * lane, near, far, far, far, None, None, None, weighted, residues * far]
    for at, block in enumerate(blocks):
        tables[c, at * STATE : (at + 1) * STATE] = far_lag if block is None else block.astype(BF16)


def mix_channels(group, rows, gains, bands, tables, projf, projr, gradf, small, skips, outs):
    lower = iota((CHUNK, CHUNK), 1) <= iota((CHUNK, CHUNK), 0)
    third = iota((SHARDS, 3 * STATE), 1) < 2 * STATE
    kvs, gms, firsts = {}, {}, {}
    for c in group:
        kv = projf[:, 3 * c + 1, :] * projf[:, 3 * c + 2, :]
        gm = gradf[:, c, :] * projf[:, 3 * c, :]
        back = projr[:, 3 * c + 1, :] * projr[:, 3 * c + 2, :]
        kvs[c], gms[c] = kv, gm
        skips[c : c + 1] = jnp.sum(kv * gm, axis=0, keepdims=True)
        kv, gm, back = kv.astype(BF16), gm.astype(BF16), back.astype(BF16)
        firsts[c] = (
            mul(kv, tables[c, 3 * STATE : 6 * STATE], NT),
            mul(kv, tables[c, 6 * STATE : 9 * STATE], NT),
            mul(gm, tables[c, 0 : 3 * STATE], NT),
            mul(back, gm, TN),
            mul(kv, bands[c]),
            mul(gm, bands[c], NT),
        )
    seconds = {}
    for c in group:
        tails, tails_lag, heads, product, _, _ = firsts[c]
        step = jnp.exp(-CHUNK * jnp.exp(rows[c : c + 1, 0 : 3 * STATE]))
        states, states_lag = carry(tails, step, tails_lag, False)
        states, states_lag = before(states, False), before(states_lag, False)
        inter = jnp.sum(heads * jnp.where(third, states, states_lag), axis=0, keepdims=True)
        adjoints, _ = carry(heads[:, 0:STATE], step[:, 0:STATE], None, True)
        adjoints = before(adjoints, True)
        skewed = pltpu.roll(product, 1, 1, stride=1, stride_axis=0)
        sums = jnp.sum(jnp.where(lower, skewed, 0.0), axis=0, keepdims=True)
        wide = jnp.broadcast_to(sums, (ROWS, CHUNK)).astype(BF16)
        seconds[c] = (
            mul(states[:, 0:STATE].astype(BF16), tables[c, 9 * STATE : 10 * STATE]),
            mul(adjoints.astype(BF16), tables[c, 10 * STATE : 11 * STATE]),
            mul(wide, tables[c, 0 : 2 * STATE], NT),
            inter,
        )
    for c in group:
        conv, corr, intra, inter = seconds[c]
        gain = gains[c : c + 1]
        conv = conv + firsts[c][4] + gain * kvs[c]
        grad_mix = corr + firsts[c][5] + gain * gms[c]
        outs[:, 3 * c, :] = gradf[:, c, :] * conv
        outs[:, 3 * c + 1, :] = grad_mix * projf[:, 3 * c + 2, :]
        outs[:, 3 * c + 2, :] = grad_mix * projf[:, 3 * c + 1, :]
        small[c : c + 1, 0 : 3 * STATE] = inter
        small[c : c + 1, 0 : 2 * STATE] += intra[0:1]


def pack(outs, mine, first, last):
    for k in range(SHARDS):
        mine[first:last, k * CHUNK : (k + 1) * CHUNK] = outs[k, first:last].astype(BF16)


def finish_small(count, small, skips, tight):
    lane = iota((ROWS, CHUNK), 1)
    row = iota((ROWS, CHUNK), 0)
    summed = jnp.sum(skips[...], axis=1, keepdims=True)
    filled = jnp.where(lane == 3 * STATE, summed, small[...])
    filled = jnp.where(row < count, filled, 0.0)
    half = ROWS // 2
    upper = pltpu.roll(filled[half:], CHUNK // 2, 1)
    tight[...] = jnp.where(lane[:half] < CHUNK // 2, filled[:half], upper)


def kernel(
    count, feat, weight, gout, rates_t, residues_t, gain, every, full, shared, packed,
    wraw, wbuf, graw, gbuf, partial, parts, grads, params, cols, rows, gains, bands,
    tables, projf, projr, gradf, outs, small, skips, gain_in, gain_got, mine, tight,
    local_sem, f_send, f_recv, r_send, r_recv, g_send, g_recv, p_send, p_recv, a_send, a_recv,
    s_send, s_recv, hello, k_send, k_recv, store_sem,
):
    seq, ch = lax.axis_index("seq"), lax.axis_index("ch")
    x, z = seq // SIDE, seq % SIDE
    y, core = ch // 2, ch % 2
    home = seq // 2
    at_home = ch == home

    feat_in = pltpu.make_async_copy(feat, every.at[seq], local_sem.at[0])
    weight_in = pltpu.make_async_copy(weight, wraw, local_sem.at[1])
    grads_in = pltpu.make_async_copy(gout, graw, local_sem.at[2])
    small_in = [
        pltpu.make_async_copy(rates_t, packed.at[pl.ds(0, STATE)], local_sem.at[3]),
        pltpu.make_async_copy(residues_t, packed.at[pl.ds(STATE, STATE)], local_sem.at[4]),
        pltpu.make_async_copy(gain, gain_in, local_sem.at[5]),
    ]
    feat_in.start()
    for copy in small_in:
        copy.start()
    weight_in.start()
    grads_in.start()

    def ring(value, step):
        return (value + step + SIDE) % SIDE

    def place(v, p, q):
        return p * SIDE + q if v == 0 else q * SIDE + p

    def spot(v):
        return (x, z) if v == 0 else (z, x)

    barrier = pltpu.get_barrier_semaphore()

    def greet(s, c):
        pl.semaphore_signal(barrier, inc=1, device_id={"seq": s, "ch": c}, device_id_type=MESH)

    for v in range(2):
        p, q = spot(v)
        for step in (-1, 1):
            greet(place(v, ring(p, step), q), ch)
    for i in range(1, WAYS):
        greet(seq, (ch + i) % WAYS)
    small[...] = jnp.zeros_like(small)
    skips[...] = jnp.zeros_like(skips)
    outs[:, TRIO - 1, :] = jnp.zeros((SHARDS, CHUNK), F32)
    pl.semaphore_wait(barrier, 4 + WAYS - 1)

    half, quarter = CHUNK // 2, CHUNK // 4
    offs = (0, -1, 1, 2)

    def piece(v, part):
        start = v * half + (quarter if part == "b" else 0)
        return pl.ds(start, half if part == "h" else quarter)

    names = [("P1+", "h"), ("P1-", "h"), ("P2+", "a"), ("P2-", "b")]
    for j in range(3):
        names += [(f"Q1+{j}", "h"), (f"Q1-{j}", "h"), (f"Q2+{j}", "a"), (f"Q2-{j}", "b")]
    names += [("Q1+3a", "a"), ("Q1+3b", "b"), ("Q1-3a", "a"), ("Q1-3b", "b")]
    names += [("Q2+3", "a"), ("Q2-3", "b")]
    number = {name: n for n, (name, _) in enumerate(names)}
    piece_of = dict(names)

    def feature_copy(v, name, arriving):
        p, q = spot(v)
        step = 1 if name[2] == "+" else -1
        hops = int(name[1]) - 1 + (1 if arriving else 0)
        if name[0] == "P":
            source = place(v, ring(p, -step * hops), q)
            target = place(v, ring(p, step), q)
        else:
            source = place(v, ring(p, offs[int(name[3])]), ring(q, -step * hops))
            target = place(v, p, ring(q, step))
        rows = piece(v, piece_of[name])
        return pltpu.make_async_remote_copy(
            src_ref=every.at[source, rows],
            dst_ref=every.at[source, rows],
            send_sem=f_send.at[v, number[name]],
            recv_sem=f_recv.at[v, number[name]],
            device_id={"seq": target},
            device_id_type=MESH,
        )

    def send(v, name):
        feature_copy(v, name, False).start()

    def arrive(v, name):
        feature_copy(v, name, True).wait_recv()

    def hello_round(n):
        for v in range(2):
            p, q = spot(v)
            for step in (-1, 1):
                pl.semaphore_signal(
                    hello.at[n],
                    inc=1,
                    device_id={"seq": place(v, ring(p, step), q)},
                    device_id_type=MESH,
                )

    def hello_wait(n):
        pl.semaphore_wait(hello.at[n], 4)

    def owner_copy(shard, i, batch):
        target = (ch + i) % WAYS
        return pltpu.make_async_remote_copy(
            src_ref=partial.at[shard, target],
            dst_ref=parts.at[i, shard],
            send_sem=r_send.at[batch, i],
            recv_sem=r_recv.at[batch, i],
            device_id={"ch": target},
            device_id_type=MESH,
        )

    def shard_at(dx, dz):
        return ring(x, dx) * SIDE + ring(z, dz)

    def project(dx, dz):
        shard = shard_at(dx, dz)
        out = mul(wbuf[...], every[shard], NT).astype(BF16).reshape(WAYS, TRIO, CHUNK)
        partial[shard] = out
        parts[0, shard] = partial[shard, ch]
        return shard

    def deliver(at):
        for i in range(1, WAYS):
            owner_copy(done[at], i, 0 if at < SHARDS - LATE else 1).start()

    def await_batch(batch, sems):
        size = LATE if batch else SHARDS - LATE
        for i in range(1, WAYS):
            block_of = parts.at[i, pl.ds(0, size)]
            pltpu.make_async_copy(block_of, block_of, sems.at[batch, i]).wait()

    feat_in.wait()
    for v in range(2):
        send(v, "P1+")
        send(v, "P1-")
    for v in range(2):
        send(v, "Q1+0")
        send(v, "Q1-0")
    hello_round(0)

    def param_copy(i):
        return pltpu.make_async_remote_copy(
            src_ref=packed,
            dst_ref=params,
            send_sem=p_send.at[i],
            recv_sem=p_recv,
            device_id={"ch": (ch + i) % WAYS},
            device_id_type=MESH,
        )

    def gain_copy(i):
        return pltpu.make_async_remote_copy(
            src_ref=gain_in,
            dst_ref=gain_got,
            send_sem=k_send.at[i],
            recv_sem=k_recv,
            device_id={"ch": (ch + i) % WAYS},
            device_id_type=MESH,
        )

    for copy in small_in:
        copy.wait()

    @pl.when(at_home)
    def _():
        pltpu.make_async_copy(packed, params, p_recv).start()
        pltpu.make_async_copy(gain_in, gain_got, k_recv).start()
        for i in range(1, WAYS):
            param_copy(i).start()
            gain_copy(i).start()

    def grad_copy(shard, c):
        slot = (shard % 2) * WAYS + c
        return pltpu.make_async_remote_copy(
            src_ref=gbuf.at[slot],
            dst_ref=grads.at[seq],
            send_sem=g_send.at[slot],
            recv_sem=g_recv,
            device_id={"seq": shard, "ch": c},
            device_id_type=MESH,
        )

    def is_self(i):
        return jnp.logical_and(2 * ch + i // WAYS == seq, i % WAYS == ch)

    def give_grads(i, _):
        @pl.when(is_self(i))
        def _():
            pltpu.make_async_copy(gbuf.at[i], grads.at[seq], g_recv).start()

        @pl.when(jnp.logical_not(is_self(i)))
        def _():
            grad_copy(2 * ch + i // WAYS, i % WAYS).start()

        return 0

    weight_in.wait()
    block = count * WAYS
    ordered = None
    for g in range(3):
        pick = chosen(
            (WAYS * TRIO, block),
            lambda r, c: (r % TRIO == 3 * (c % count) + g) & (r // TRIO == c // count),
        )
        part = mul(pick, wraw[g])
        ordered = part if ordered is None else ordered + part
    wbuf[...] = ordered.astype(BF16)
    grads_in.wait()
    pick = chosen(
        (2 * WAYS * ROWS, 2 * block), lambda r, c: (r // ROWS == c // count) & (r % ROWS == c % count)
    )
    gbuf[...] = mul(pick, graw[...]).astype(BF16).reshape(2 * WAYS, ROWS, CHUNK)

    hello_wait(0)
    hello_round(1)
    done = [project(0, 0)]
    hello_wait(1)
    hello_round(2)
    hello_wait(2)
    hello_round(3)

    def follow(dx, dz):
        done.append(project(dx, dz))
        deliver(len(done) - 2)

    prepared = []

    def prepare(number_of):
        for _ in range(number_of):
            if len(prepared) < count:
                tables_of(len(prepared), cols, bands, tables)
                prepared.append(0)

    hello_wait(3)
    arrive(0, "P1+")
    send(0, "P2+")
    send(0, "Q1+1")
    send(0, "Q1-1")
    pltpu.make_async_copy(packed, params, p_recv).wait()
    pltpu.make_async_copy(gain_in, gain_got, k_recv).wait()
    offset = (seq % 2) * block + ch * count
    select_params(count, offset, params, gain_got, cols, rows, gains)
    arrive(0, "P1-")
    send(0, "P2-")
    send(0, "Q1+2")
    send(0, "Q1-2")
    prepare(1)
    arrive(1, "P1+")
    send(1, "P2+")
    send(1, "Q1+1")
    send(1, "Q1-1")
    prepare(1)
    arrive(1, "P1-")
    send(1, "P2-")
    send(1, "Q1+2")
    send(1, "Q1-2")
    prepare(1)
    arrive(0, "Q1+0")
    send(0, "Q2+0")
    follow(0, -1)
    prepare(1)
    arrive(0, "Q1-0")
    send(0, "Q2-0")
    follow(0, 1)
    prepare(1)
    arrive(1, "Q1+0")
    send(1, "Q2+0")
    follow(-1, 0)
    prepare(1)
    arrive(1, "Q1-0")
    send(1, "Q2-0")
    follow(1, 0)
    prepare(1)
    arrive(0, "P2+")
    send(0, "Q1+3a")
    send(0, "Q1-3a")
    prepare(1)
    arrive(0, "P2-")
    send(0, "Q1+3b")
    send(0, "Q1-3b")
    arrive(0, "Q1+1")
    arrive(0, "Q1-1")
    arrive(1, "Q1+1")
    arrive(1, "Q1-1")
    arrive(0, "Q1+2")
    arrive(0, "Q1-2")
    follow(-1, -1)
    follow(1, -1)
    prepare(1)
    arrive(1, "P2+")
    send(1, "Q1+3a")
    send(1, "Q1-3a")
    prepare(1)
    arrive(1, "P2-")
    send(1, "Q1+3b")
    send(1, "Q1-3b")
    send(0, "Q2+1")
    send(0, "Q2-1")
    send(1, "Q2+1")
    send(1, "Q2-1")
    send(0, "Q2+2")
    send(0, "Q2-2")
    prepare(1)
    arrive(1, "Q1+2")
    send(1, "Q2+2")
    follow(-1, 1)
    prepare(1)
    arrive(1, "Q1-2")
    send(1, "Q2-2")
    arrive(1, "Q2+0")
    arrive(1, "Q2-0")
    arrive(0, "Q2+0")
    arrive(0, "Q2-0")
    follow(1, 1)
    follow(2, 0)
    follow(0, 2)
    prepare(1)
    arrive(0, "Q1+3a")
    send(0, "Q2+3")
    arrive(0, "Q1-3a")
    arrive(1, "Q1+3a")
    prepare(1)
    arrive(0, "Q1-3b")
    send(0, "Q2-3")
    send(1, "Q2+3")
    arrive(1, "Q1-3a")
    arrive(0, "Q1+3b")
    prepare(1)
    arrive(1, "Q1-3b")
    send(1, "Q2-3")
    lax.fori_loop(0, SHARDS, give_grads, 0)
    arrive(1, "Q1+3b")
    arrive(0, "Q2+1")
    arrive(0, "Q2-1")
    follow(-1, 2)
    arrive(1, "Q2+1")
    arrive(1, "Q2-1")
    follow(2, -1)
    arrive(0, "Q2+2")
    arrive(0, "Q2-2")
    follow(1, 2)
    arrive(1, "Q2+2")
    arrive(1, "Q2-2")
    follow(2, 1)
    arrive(0, "Q2+3")
    arrive(0, "Q2-3")
    arrive(1, "Q2+3")
    arrive(1, "Q2-3")
    follow(2, 2)
    deliver(SHARDS - 1)
    prepare(count)

    pltpu.make_async_copy(gbuf, grads, g_recv).wait()
    await_batch(0, r_recv)
    sum_partials(done[: SHARDS - LATE], parts, grads, projf, projr, gradf)
    await_batch(1, r_recv)
    sum_partials(done[SHARDS - LATE :], parts, grads, projf, projr, gradf)

    width = SHARDS * CHUNK
    left, right = pl.ds(0, width // 2), pl.ds(width // 2, width // 2)
    whole = pl.ds(0, width)
    tiles = [pl.ds(0, 16), pl.ds(16, 16), pl.ds(32, TRIO - 32)]
    straight = (False, False, True)

    def owner(step, other):
        return ring(y, step) * 2 + (1 - core if other else core)

    def group_copy(t, n, slot, target, lanes, own):
        return pltpu.make_async_remote_copy(
            src_ref=mine.at[tiles[t], lanes] if own else full.at[slot, tiles[t], lanes],
            dst_ref=full.at[slot, tiles[t], lanes],
            send_sem=a_send.at[t, n],
            recv_sem=a_recv.at[t, n],
            device_id={"ch": target},
            device_id_type=MESH,
        )

    relayed = {
        0: (0, 1, False, whole),
        1: (0, -1, False, whole),
        2: (0, 0, True, whole),
        3: (1, 1, False, left),
        4: (-1, -1, False, right),
        5: (1, 0, True, whole),
        6: (-1, 0, True, whole),
        7: (2, 0, True, left),
        8: (2, 0, True, right),
    }
    direct = {n: relayed[n] for n in (0, 1, 2, 5, 6)}
    direct[3] = (0, 2, False, whole)
    direct[7] = (2, 0, True, whole)
    kinds = [direct if straight[t] else relayed for t in range(3)]

    def going(t, n):
        back, step, other, lanes = kinds[t][n]
        return group_copy(t, n, owner(-back, False), owner(step, other), lanes, back == 0)

    def coming(t, n):
        back, step, other, lanes = kinds[t][n]
        return group_copy(t, n, owner(-back - step, other), owner(step, other), lanes, False)

    def own_copy(t):
        return pltpu.make_async_copy(
            mine.at[tiles[t]], full.at[ch, tiles[t]], store_sem.at[t]
        )

    def begin(t):
        for n in (0, 1, 3, 2) if straight[t] else (0, 1, 2):
            going(t, n).start()
        own_copy(t).start()

    def relay(t):
        coming(t, 0).wait_recv()
        if not straight[t]:
            going(t, 3).start()
        going(t, 5).start()
        coming(t, 1).wait_recv()
        if not straight[t]:
            going(t, 4).start()
        going(t, 6).start()

    def relay_far(t):
        coming(t, 3).wait_recv()
        going(t, 7).start()
        if not straight[t]:
            coming(t, 4).wait_recv()
            going(t, 8).start()

    def small_copy(i):
        return pltpu.make_async_remote_copy(
            src_ref=tight,
            dst_ref=shared.at[(seq % 2) * WAYS + ch],
            send_sem=s_send.at[i],
            recv_sem=s_recv,
            device_id={"seq": i, "ch": home},
            device_id_type=MESH,
        )

    def small_self(i):
        return jnp.logical_and(i == seq, at_home)

    def start_small(i, _):
        @pl.when(small_self(i))
        def _():
            pltpu.make_async_copy(tight, shared.at[(seq % 2) * WAYS + ch], s_recv).start()

        @pl.when(jnp.logical_not(small_self(i)))
        def _():
            small_copy(i).start()

        return 0

    groups = [range(0, 6), range(6, 11), range(11, count)]
    edges = [(0, 16), (16, 32), (32, TRIO)]
    for t in range(3):
        mix_channels(
            groups[t], rows, gains, bands, tables, projf, projr, gradf, small, skips, outs
        )
        pack(outs, mine, *edges[t])
        begin(t)
    finish_small(count, small, skips, tight)
    relay(0)
    lax.fori_loop(0, SHARDS, start_small, 0)
    relay(1)
    relay_far(0)
    relay(2)
    relay_far(1)
    relay_far(2)

    for v in range(2):
        for name, _ in names:
            feature_copy(v, name, False).wait_send()
    await_batch(0, r_send)
    await_batch(1, r_send)

    def end_sends(i, _):
        @pl.when(jnp.logical_not(is_self(i)))
        def _():
            grad_copy(2 * ch + i // WAYS, i % WAYS).wait_send()

        @pl.when(jnp.logical_not(small_self(i)))
        def _():
            small_copy(i).wait_send()

        return 0

    lax.fori_loop(0, SHARDS, end_sends, 0)

    @pl.when(at_home)
    def _():
        for i in range(1, WAYS):
            param_copy(i).wait_send()
            gain_copy(i).wait_send()

    for t in range(3):
        own_copy(t).wait()
        for n in kinds[t]:
            going(t, n).wait_send()
            if n in (2, 5, 6, 7, 8):
                coming(t, n).wait_recv()
    pltpu.make_async_copy(shared, shared, s_recv).wait()


def finish(
    count, features, full, shared, packed, wgrad, residue_out, rate_out, skip_out, rows
):
    block = count * WAYS
    tokens = full.shape[2]
    width = wgrad.shape[2]
    lanes = pl.ds(pl.multiple_of(pl.program_id(0) * width, width), width)
    right_side = features[:, :, lanes].reshape(tokens, width)
    product = mul(full[...].reshape(WAYS * TRIO, tokens), right_side)
    for part in range(rows.shape[0]):
        lanes = pl.ds(part * CHUNK, CHUNK)
        rows[part] = product[:, part * CHUNK : (part + 1) * CHUNK]
        for owner in range(WAYS):
            for g in range(3):
                own = rows[part, pl.ds(owner * TRIO + g, count, stride=3), :]
                wgrad[g, owner * count : (owner + 1) * count, lanes] = own

    @pl.when(pl.program_id(0) == 0)
    def _():
        half = ROWS // 2
        tiles = shared[...].reshape(2 * WAYS * half, CHUNK)
        turned = []
        for first in (0, half):
            pick = chosen(
                (2 * WAYS * half, 2 * block),
                lambda r, c: (r // half == c // count) & (r % half + first == c % count),
                F32,
            )
            turned.append(exact(tiles, pick, TN))
        turned = turned[0][: CHUNK // 2] + turned[1][CHUNK // 2 :]
        moment = turned[STATE : 2 * STATE] + turned[2 * STATE : 3 * STATE]
        residue_out[...] = turned[0:STATE]
        rate_out[...] = -packed[STATE:] * jnp.exp(packed[0:STATE]) * moment
        skip_out[...] = turned[3 * STATE : 3 * STATE + 1]


def local(features, qkv_weight, grad_out, residues, log_rates, skip_gain):
    width = features.shape[1]
    block = qkv_weight.shape[0]
    count = block // WAYS
    held, order = residues.shape
    weight = qkv_weight.transpose(1, 0, 2)
    anywhere = pl.BlockSpec(memory_space=pl.ANY)
    vmem = pl.BlockSpec(memory_space=pltpu.VMEM)
    dma = pltpu.SemaphoreType.DMA
    tokens = SHARDS * CHUNK
    operands = [
        pltpu.with_memory_space_constraint(array, pltpu.MemorySpace.HBM)
        for array in (
            features, weight, grad_out, log_rates.T, residues.T, skip_gain.reshape(1, held)
        )
    ]
    every, full, shared, packed = pl.pallas_call(
        functools.partial(kernel, count),
        out_shape=(
            jax.ShapeDtypeStruct((SHARDS, CHUNK, width), BF16),
            jax.ShapeDtypeStruct((WAYS, TRIO, tokens), BF16),
            jax.ShapeDtypeStruct((2 * WAYS, ROWS // 2, CHUNK), F32),
            jax.ShapeDtypeStruct((PARAM_ROWS, held), F32),
        ),
        in_specs=[anywhere] * 6,
        out_specs=(vmem,) * 4,
        scratch_shapes=[
            pltpu.VMEM((3, block, width), BF16),
            pltpu.VMEM((WAYS * TRIO, width), BF16),
            pltpu.VMEM((held, CHUNK), BF16),
            pltpu.VMEM((2 * WAYS, ROWS, CHUNK), BF16),
            pltpu.VMEM((SHARDS, WAYS, TRIO, CHUNK), BF16),
            pltpu.VMEM((WAYS, SHARDS, TRIO, CHUNK), BF16),
            pltpu.VMEM((SHARDS, ROWS, CHUNK), BF16),
            pltpu.VMEM((PARAM_ROWS, held), F32),
            pltpu.VMEM((2 * STATE, CHUNK), F32),
            pltpu.VMEM((ROWS, CHUNK), F32),
            pltpu.VMEM((ROWS, CHUNK), F32),
            pltpu.VMEM((ROWS, CHUNK, CHUNK), BF16),
            pltpu.VMEM((ROWS, 11 * STATE, CHUNK), BF16),
            pltpu.VMEM((SHARDS, TRIO, CHUNK), F32),
            pltpu.VMEM((SHARDS, TRIO, CHUNK), F32),
            pltpu.VMEM((SHARDS, ROWS, CHUNK), F32),
            pltpu.VMEM((SHARDS, TRIO, CHUNK), F32),
            pltpu.VMEM((ROWS, CHUNK), F32),
            pltpu.VMEM((ROWS, CHUNK), F32),
            pltpu.VMEM((1, held), F32),
            pltpu.VMEM((1, held), F32),
            pltpu.VMEM((TRIO, tokens), BF16),
            pltpu.VMEM((ROWS // 2, CHUNK), F32),
            dma((6,)),
            dma((2, 22)),
            dma((2, 22)),
            dma((2, WAYS)),
            dma((2, WAYS)),
            dma((SHARDS,)),
            dma,
            dma((WAYS,)),
            dma,
            dma((3, 9)),
            dma((3, 9)),
            dma((SHARDS,)),
            dma,
            pltpu.SemaphoreType.REGULAR((4,)),
            dma((WAYS,)),
            dma,
            dma((3,)),
        ],
        compiler_params=pltpu.CompilerParams(
            collective_id=0, has_side_effects=True, vmem_limit_bytes=24 * 2**20
        ),
    )(*operands)
    columns = 512

    def same(*shape):
        return pl.BlockSpec(shape, lambda n: (0,) * len(shape))

    weight_grad, residue_grad, rate_grad, skip_grad = pl.pallas_call(
        functools.partial(finish, count),
        grid=(width // columns,),
        out_shape=(
            jax.ShapeDtypeStruct((3, block, width), F32),
            jax.ShapeDtypeStruct((order, held), F32),
            jax.ShapeDtypeStruct((order, held), F32),
            jax.ShapeDtypeStruct((1, held), F32),
        ),
        in_specs=[
            vmem,
            vmem,
            vmem,
            vmem,
        ],
        out_specs=(
            pl.BlockSpec((3, block, columns), lambda n: (0, 0, n)),
            same(order, held),
            same(order, held),
            same(1, held),
        ),
        scratch_shapes=[pltpu.VMEM((columns // CHUNK, WAYS * TRIO, CHUNK), F32)],
        compiler_params=pltpu.CompilerParams(vmem_limit_bytes=24 * 2**20),
    )(every, full, shared, packed)
    return weight_grad.transpose(1, 0, 2), residue_grad.T, rate_grad.T, skip_grad.reshape(held)


def solution(mesh):
    placed = (
        P("seq", "ch"),
        P("seq", None, "ch"),
        P("ch", "seq"),
        P("ch", None),
        P("ch", None),
        P("ch"),
    )
    return jax.shard_map(
        local,
        mesh=mesh,
        in_specs=placed,
        out_specs=(P("seq", None, "ch"), P("ch", None), P("ch", None), P("ch")),
        check_vma=False,
    )
```

```python
import functools

import jax
import jax.numpy as jnp
from jax import lax
from jax.experimental import pallas as pl
from jax.experimental.pallas import tpu as pltpu
from jax.sharding import PartitionSpec as P

F32, BF16 = jnp.float32, jnp.bfloat16
CHUNK = 128
SIDE = 4
SHARDS = SIDE * SIDE
WAYS = 2 * SIDE
ROWS = 16
TRIO = 40
STATE = 16
LATE = 5
MESH = pl.DeviceIdType.MESH
PARAM_ROWS = 2 * STATE

NT = (((1,), (1,)), ((), ()))
TN = (((0,), (0,)), ((), ()))
NN = (((1,), (0,)), ((), ()))


def mul(a, b, dims=NN):
    return lax.dot_general(a, b, dims, preferred_element_type=F32)


def exact(a, b, dims=NN):
    return lax.dot_general(a, b, dims, precision="highest", preferred_element_type=F32)


def iota(shape, dim):
    return lax.broadcasted_iota(jnp.int32, shape, dim)


def chosen(shape, rule, kind=BF16):
    return rule(iota(shape, 0), iota(shape, 1)).astype(kind)


def sum_partials(shards, parts, grads, projf, projr, gradf):
    flip = chosen((CHUNK, CHUNK), lambda r, c: r + c == CHUNK - 1)
    for k in shards:
        total = parts[0, k].astype(F32)
        for way in range(1, WAYS):
            total = total + parts[way, k].astype(F32)
        rounded = total.astype(BF16)
        projf[k] = rounded.astype(F32)
        projr[k] = mul(rounded, flip)
        gradf[k] = grads[k].astype(F32)


def carry(values, step, lagged, reverse):
    row = iota(values.shape, 0)
    shape = values.shape
    decay = jnp.broadcast_to(step, shape)
    reach = 1
    while reach < shape[0]:
        amount = shape[0] - reach if reverse else reach
        keep = row < shape[0] - reach if reverse else row >= reach
        near = jnp.where(keep, decay * pltpu.roll(values, amount, 0), 0.0)
        if lagged is not None:
            moved = jnp.where(keep, decay * pltpu.roll(lagged, amount, 0), 0.0)
            lagged = lagged + moved + (CHUNK * reach) * near
        values = values + near
        decay = decay * decay
        reach *= 2
    return values, lagged


def before(values, reverse):
    row = iota(values.shape, 0)
    last = values.shape[0] - 1
    if reverse:
        return jnp.where(row < last, pltpu.roll(values, last, 0), 0.0)
    return jnp.where(row >= 1, pltpu.roll(values, 1, 0), 0.0)


def select_params(count, offset, params, gain, cols, rows, gains):
    lanes = params.shape[1]
    down = chosen((lanes, CHUNK), lambda r, c: (r == c + offset) & (c < count), F32)
    across = chosen((ROWS, lanes), lambda r, c: (c == r + offset) & (r < count), F32)
    cols[...] = exact(params[0 : 2 * STATE], down)
    rates = params[0:STATE]
    rows[:, 0 : 3 * STATE] = exact(across, jnp.concatenate([rates, rates, rates], 0), NT)
    gains[...] = exact(across, jnp.broadcast_to(gain[...], (CHUNK, lanes)), NT)


def tables_of(c, cols, bands, tables):
    lane = iota((STATE, CHUNK), 1).astype(F32)
    rates = jnp.exp(cols[0:STATE, c : c + 1])
    residues = cols[STATE : 2 * STATE, c : c + 1]
    near = jnp.exp(-rates * lane)
    far = jnp.exp(-rates * (CHUNK - lane))
    weighted = residues * near
    taps = jnp.sum(weighted, axis=0, keepdims=True)
    upper = iota((CHUNK, CHUNK), 1) >= iota((CHUNK, CHUNK), 0)
    spread = pltpu.roll(jnp.broadcast_to(taps, (CHUNK, CHUNK)), 0, 1, stride=1, stride_axis=0)
    bands[c] = jnp.where(upper, spread, 0.0).astype(BF16)
    far_lag = (far * (CHUNK - lane)).astype(BF16)
    blocks = [near, near * lane, near, far, far, far, None, None, None, weighted, residues * far]
    for at, block in enumerate(blocks):
        tables[c, at * STATE : (at + 1) * STATE] = far_lag if block is None else block.astype(BF16)


def mix_channels(group, rows, gains, bands, tables, projf, projr, gradf, small, skips, outs):
    lower = iota((CHUNK, CHUNK), 1) <= iota((CHUNK, CHUNK), 0)
    third = iota((SHARDS, 3 * STATE), 1) < 2 * STATE
    kvs, gms, firsts = {}, {}, {}
    for c in group:
        kv = projf[:, 3 * c + 1, :] * projf[:, 3 * c + 2, :]
        gm = gradf[:, c, :] * projf[:, 3 * c, :]
        back = projr[:, 3 * c + 1, :] * projr[:, 3 * c + 2, :]
        kvs[c], gms[c] = kv, gm
        skips[c : c + 1] = jnp.sum(kv * gm, axis=0, keepdims=True)
        kv, gm, back = kv.astype(BF16), gm.astype(BF16), back.astype(BF16)
        firsts[c] = (
            mul(kv, tables[c, 3 * STATE : 6 * STATE], NT),
            mul(kv, tables[c, 6 * STATE : 9 * STATE], NT),
            mul(gm, tables[c, 0 : 3 * STATE], NT),
            mul(back, gm, TN),
            mul(kv, bands[c]),
            mul(gm, bands[c], NT),
        )
    seconds = {}
    for c in group:
        tails, tails_lag, heads, product, _, _ = firsts[c]
        step = jnp.exp(-CHUNK * jnp.exp(rows[c : c + 1, 0 : 3 * STATE]))
        states, states_lag = carry(tails, step, tails_lag, False)
        states, states_lag = before(states, False), before(states_lag, False)
        inter = jnp.sum(heads * jnp.where(third, states, states_lag), axis=0, keepdims=True)
        adjoints, _ = carry(heads[:, 0:STATE], step[:, 0:STATE], None, True)
        adjoints = before(adjoints, True)
        skewed = pltpu.roll(product, 1, 1, stride=1, stride_axis=0)
        sums = jnp.sum(jnp.where(lower, skewed, 0.0), axis=0, keepdims=True)
        wide = jnp.broadcast_to(sums, (ROWS, CHUNK)).astype(BF16)
        seconds[c] = (
            mul(states[:, 0:STATE].astype(BF16), tables[c, 9 * STATE : 10 * STATE]),
            mul(adjoints.astype(BF16), tables[c, 10 * STATE : 11 * STATE]),
            mul(wide, tables[c, 0 : 2 * STATE], NT),
            inter,
        )
    for c in group:
        conv, corr, intra, inter = seconds[c]
        gain = gains[c : c + 1]
        conv = conv + firsts[c][4] + gain * kvs[c]
        grad_mix = corr + firsts[c][5] + gain * gms[c]
        outs[:, 3 * c, :] = gradf[:, c, :] * conv
        outs[:, 3 * c + 1, :] = grad_mix * projf[:, 3 * c + 2, :]
        outs[:, 3 * c + 2, :] = grad_mix * projf[:, 3 * c + 1, :]
        small[c : c + 1, 0 : 3 * STATE] = inter
        small[c : c + 1, 0 : 2 * STATE] += intra[0:1]


def pack(outs, mine, first, last):
    for k in range(SHARDS):
        mine[first:last, k * CHUNK : (k + 1) * CHUNK] = outs[k, first:last].astype(BF16)


def finish_small(count, small, skips, tight):
    lane = iota((ROWS, CHUNK), 1)
    row = iota((ROWS, CHUNK), 0)
    summed = jnp.sum(skips[...], axis=1, keepdims=True)
    filled = jnp.where(lane == 3 * STATE, summed, small[...])
    filled = jnp.where(row < count, filled, 0.0)
    half = ROWS // 2
    upper = pltpu.roll(filled[half:], CHUNK // 2, 1)
    tight[...] = jnp.where(lane[:half] < CHUNK // 2, filled[:half], upper)


def kernel(
    count, feat, weight, gout, rates_t, residues_t, gain, every, full, shared, packed,
    wraw, wbuf, graw, gbuf, partial, parts, grads, params, cols, rows, gains, bands,
    tables, projf, projr, gradf, outs, small, skips, gain_in, gain_got, mine, tight,
    local_sem, f_send, f_recv, r_send, r_recv, g_send, g_recv, p_send, p_recv, a_send, a_recv,
    s_send, s_recv, hello, k_send, k_recv, store_sem,
):
    seq, ch = lax.axis_index("seq"), lax.axis_index("ch")
    x, z = seq // SIDE, seq % SIDE
    y, core = ch // 2, ch % 2
    home = seq // 2
    at_home = ch == home

    feat_in = pltpu.make_async_copy(feat, every.at[seq], local_sem.at[0])
    weight_in = pltpu.make_async_copy(weight, wraw, local_sem.at[1])
    grads_in = pltpu.make_async_copy(gout, graw, local_sem.at[2])
    small_in = [
        pltpu.make_async_copy(rates_t, packed.at[pl.ds(0, STATE)], local_sem.at[3]),
        pltpu.make_async_copy(residues_t, packed.at[pl.ds(STATE, STATE)], local_sem.at[4]),
        pltpu.make_async_copy(gain, gain_in, local_sem.at[5]),
    ]
    feat_in.start()
    for copy in small_in:
        copy.start()
    weight_in.start()
    grads_in.start()

    def ring(value, step):
        return (value + step + SIDE) % SIDE

    def place(v, p, q):
        return p * SIDE + q if v == 0 else q * SIDE + p

    def spot(v):
        return (x, z) if v == 0 else (z, x)

    barrier = pltpu.get_barrier_semaphore()

    def greet(s, c):
        pl.semaphore_signal(barrier, inc=1, device_id={"seq": s, "ch": c}, device_id_type=MESH)

    for v in range(2):
        p, q = spot(v)
        for step in (-1, 1):
            greet(place(v, ring(p, step), q), ch)
    for i in range(1, WAYS):
        greet(seq, (ch + i) % WAYS)
    small[...] = jnp.zeros_like(small)
    skips[...] = jnp.zeros_like(skips)
    outs[:, TRIO - 1, :] = jnp.zeros((SHARDS, CHUNK), F32)
    pl.semaphore_wait(barrier, 4 + WAYS - 1)

    half, quarter = CHUNK // 2, CHUNK // 4
    offs = (0, -1, 1, 2)

    def piece(v, part):
        start = v * half + (quarter if part == "b" else 0)
        return pl.ds(start, half if part == "h" else quarter)

    names = [("P1+", "h"), ("P1-", "h"), ("P2+", "a"), ("P2-", "b")]
    for j in range(3):
        names += [(f"Q1+{j}", "h"), (f"Q1-{j}", "h"), (f"Q2+{j}", "a"), (f"Q2-{j}", "b")]
    names += [("Q1+3a", "a"), ("Q1+3b", "b"), ("Q1-3a", "a"), ("Q1-3b", "b")]
    names += [("Q2+3", "a"), ("Q2-3", "b")]
    number = {name: n for n, (name, _) in enumerate(names)}
    piece_of = dict(names)

    def feature_copy(v, name, arriving):
        p, q = spot(v)
        step = 1 if name[2] == "+" else -1
        hops = int(name[1]) - 1 + (1 if arriving else 0)
        if name[0] == "P":
            source = place(v, ring(p, -step * hops), q)
            target = place(v, ring(p, step), q)
        else:
            source = place(v, ring(p, offs[int(name[3])]), ring(q, -step * hops))
            target = place(v, p, ring(q, step))
        rows = piece(v, piece_of[name])
        return pltpu.make_async_remote_copy(
            src_ref=every.at[source, rows],
            dst_ref=every.at[source, rows],
            send_sem=f_send.at[v, number[name]],
            recv_sem=f_recv.at[v, number[name]],
            device_id={"seq": target},
            device_id_type=MESH,
        )

    def send(v, name):
        feature_copy(v, name, False).start()

    def arrive(v, name):
        feature_copy(v, name, True).wait_recv()

    def hello_round(n):
        for v in range(2):
            p, q = spot(v)
            for step in (-1, 1):
                pl.semaphore_signal(
                    hello.at[n],
                    inc=1,
                    device_id={"seq": place(v, ring(p, step), q)},
                    device_id_type=MESH,
                )

    def hello_wait(n):
        pl.semaphore_wait(hello.at[n], 4)

    def owner_copy(shard, i, batch):
        target = (ch + i) % WAYS
        return pltpu.make_async_remote_copy(
            src_ref=partial.at[shard, target],
            dst_ref=parts.at[i, shard],
            send_sem=r_send.at[batch, i],
            recv_sem=r_recv.at[batch, i],
            device_id={"ch": target},
            device_id_type=MESH,
        )

    def shard_at(dx, dz):
        return ring(x, dx) * SIDE + ring(z, dz)

    def project(dx, dz):
        shard = shard_at(dx, dz)
        out = mul(wbuf[...], every[shard], NT).astype(BF16).reshape(WAYS, TRIO, CHUNK)
        partial[shard] = out
        parts[0, shard] = partial[shard, ch]
        return shard

    def deliver(at):
        for i in range(1, WAYS):
            owner_copy(done[at], i, 0 if at < SHARDS - LATE else 1).start()

    def await_batch(batch, sems):
        size = LATE if batch else SHARDS - LATE
        for i in range(1, WAYS):
            block_of = parts.at[i, pl.ds(0, size)]
            pltpu.make_async_copy(block_of, block_of, sems.at[batch, i]).wait()

    feat_in.wait()
    for v in range(2):
        send(v, "P1+")
        send(v, "P1-")
    for v in range(2):
        send(v, "Q1+0")
        send(v, "Q1-0")
    hello_round(0)

    def param_copy(i):
        return pltpu.make_async_remote_copy(
            src_ref=packed,
            dst_ref=params,
            send_sem=p_send.at[i],
            recv_sem=p_recv,
            device_id={"ch": (ch + i) % WAYS},
            device_id_type=MESH,
        )

    def gain_copy(i):
        return pltpu.make_async_remote_copy(
            src_ref=gain_in,
            dst_ref=gain_got,
            send_sem=k_send.at[i],
            recv_sem=k_recv,
            device_id={"ch": (ch + i) % WAYS},
            device_id_type=MESH,
        )

    for copy in small_in:
        copy.wait()

    @pl.when(at_home)
    def _():
        pltpu.make_async_copy(packed, params, p_recv).start()
        pltpu.make_async_copy(gain_in, gain_got, k_recv).start()
        for i in range(1, WAYS):
            param_copy(i).start()
            gain_copy(i).start()

    def grad_copy(shard, c):
        slot = (shard % 2) * WAYS + c
        return pltpu.make_async_remote_copy(
            src_ref=gbuf.at[slot],
            dst_ref=grads.at[seq],
            send_sem=g_send.at[slot],
            recv_sem=g_recv,
            device_id={"seq": shard, "ch": c},
            device_id_type=MESH,
        )

    def is_self(i):
        return jnp.logical_and(2 * ch + i // WAYS == seq, i % WAYS == ch)

    def give_grads(i, _):
        @pl.when(is_self(i))
        def _():
            pltpu.make_async_copy(gbuf.at[i], grads.at[seq], g_recv).start()

        @pl.when(jnp.logical_not(is_self(i)))
        def _():
            grad_copy(2 * ch + i // WAYS, i % WAYS).start()

        return 0

    weight_in.wait()
    block = count * WAYS
    ordered = None
    for g in range(3):
        pick = chosen(
            (WAYS * TRIO, block),
            lambda r, c: (r % TRIO == 3 * (c % count) + g) & (r // TRIO == c // count),
        )
        part = mul(pick, wraw[g])
        ordered = part if ordered is None else ordered + part
    wbuf[...] = ordered.astype(BF16)
    grads_in.wait()
    pick = chosen(
        (2 * WAYS * ROWS, 2 * block), lambda r, c: (r // ROWS == c // count) & (r % ROWS == c % count)
    )
    gbuf[...] = mul(pick, graw[...]).astype(BF16).reshape(2 * WAYS, ROWS, CHUNK)

    hello_wait(0)
    hello_round(1)
    done = [project(0, 0)]
    hello_wait(1)
    hello_round(2)
    hello_wait(2)
    hello_round(3)

    delivered = []

    def flush(but=0):
        while len(delivered) < len(done) - but:
            deliver(len(delivered))
            delivered.append(0)

    def follow(dx, dz):
        done.append(project(dx, dz))
        flush(1)

    prepared = []

    def prepare(number_of):
        for _ in range(number_of):
            if len(prepared) < count:
                tables_of(len(prepared), cols, bands, tables)
                prepared.append(0)

    hello_wait(3)
    arrive(0, "P1+")
    send(0, "P2+")
    send(0, "Q1+1")
    send(0, "Q1-1")
    pltpu.make_async_copy(packed, params, p_recv).wait()
    pltpu.make_async_copy(gain_in, gain_got, k_recv).wait()
    offset = (seq % 2) * block + ch * count
    select_params(count, offset, params, gain_got, cols, rows, gains)
    arrive(0, "P1-")
    send(0, "P2-")
    send(0, "Q1+2")
    send(0, "Q1-2")
    prepare(1)
    arrive(1, "P1+")
    send(1, "P2+")
    send(1, "Q1+1")
    send(1, "Q1-1")
    prepare(1)
    arrive(1, "P1-")
    send(1, "P2-")
    send(1, "Q1+2")
    send(1, "Q1-2")
    prepare(1)
    arrive(0, "Q1+0")
    send(0, "Q2+0")
    follow(0, -1)
    prepare(1)
    flush()
    arrive(0, "Q1-0")
    send(0, "Q2-0")
    follow(0, 1)
    prepare(1)
    flush()
    arrive(1, "Q1+0")
    send(1, "Q2+0")
    follow(-1, 0)
    prepare(1)
    flush()
    arrive(1, "Q1-0")
    send(1, "Q2-0")
    follow(1, 0)
    prepare(1)
    flush()
    arrive(0, "P2+")
    send(0, "Q1+3a")
    send(0, "Q1-3a")
    prepare(1)
    arrive(0, "P2-")
    send(0, "Q1+3b")
    send(0, "Q1-3b")
    arrive(0, "Q1+1")
    arrive(0, "Q1-1")
    arrive(1, "Q1+1")
    arrive(1, "Q1-1")
    arrive(0, "Q1+2")
    arrive(0, "Q1-2")
    follow(-1, -1)
    follow(1, -1)
    prepare(1)
    flush()
    arrive(1, "P2+")
    send(1, "Q1+3a")
    send(1, "Q1-3a")
    prepare(1)
    arrive(1, "P2-")
    send(1, "Q1+3b")
    send(1, "Q1-3b")
    send(0, "Q2+1")
    send(0, "Q2-1")
    send(1, "Q2+1")
    send(1, "Q2-1")
    send(0, "Q2+2")
    send(0, "Q2-2")
    prepare(1)
    arrive(1, "Q1+2")
    send(1, "Q2+2")
    follow(-1, 1)
    prepare(1)
    flush()
    arrive(1, "Q1-2")
    send(1, "Q2-2")
    arrive(1, "Q2+0")
    arrive(1, "Q2-0")
    arrive(0, "Q2+0")
    arrive(0, "Q2-0")
    follow(1, 1)
    follow(2, 0)
    follow(0, 2)
    prepare(1)
    flush()
    arrive(0, "Q1+3a")
    send(0, "Q2+3")
    arrive(0, "Q1-3a")
    arrive(1, "Q1+3a")
    prepare(1)
    arrive(0, "Q1-3b")
    send(0, "Q2-3")
    send(1, "Q2+3")
    arrive(1, "Q1-3a")
    arrive(0, "Q1+3b")
    prepare(1)
    arrive(1, "Q1-3b")
    send(1, "Q2-3")
    lax.fori_loop(0, SHARDS, give_grads, 0)
    arrive(1, "Q1+3b")
    arrive(0, "Q2+1")
    arrive(0, "Q2-1")
    follow(-1, 2)
    flush()
    arrive(1, "Q2+1")
    arrive(1, "Q2-1")
    follow(2, -1)
    flush()
    arrive(0, "Q2+2")
    arrive(0, "Q2-2")
    follow(1, 2)
    flush()
    arrive(1, "Q2+2")
    arrive(1, "Q2-2")
    follow(2, 1)
    flush()
    arrive(0, "Q2+3")
    arrive(0, "Q2-3")
    arrive(1, "Q2+3")
    arrive(1, "Q2-3")
    follow(2, 2)
    flush()
    prepare(count)

    pltpu.make_async_copy(gbuf, grads, g_recv).wait()
    await_batch(0, r_recv)
    sum_partials(done[: SHARDS - LATE], parts, grads, projf, projr, gradf)
    await_batch(1, r_recv)
    sum_partials(done[SHARDS - LATE :], parts, grads, projf, projr, gradf)

    width = SHARDS * CHUNK
    left, right = pl.ds(0, width // 2), pl.ds(width // 2, width // 2)
    whole = pl.ds(0, width)
    tiles = [pl.ds(0, 16), pl.ds(16, 16), pl.ds(32, TRIO - 32)]
    straight = (False, False, True)

    def owner(step, other):
        return ring(y, step) * 2 + (1 - core if other else core)

    def group_copy(t, n, slot, target, lanes, own):
        return pltpu.make_async_remote_copy(
            src_ref=mine.at[tiles[t], lanes] if own else full.at[slot, tiles[t], lanes],
            dst_ref=full.at[slot, tiles[t], lanes],
            send_sem=a_send.at[t, n],
            recv_sem=a_recv.at[t, n],
            device_id={"ch": target},
            device_id_type=MESH,
        )

    relayed = {
        0: (0, 1, False, whole),
        1: (0, -1, False, whole),
        2: (0, 0, True, whole),
        3: (1, 1, False, left),
        4: (-1, -1, False, right),
        5: (1, 0, True, whole),
        6: (-1, 0, True, whole),
        7: (2, 0, True, left),
        8: (2, 0, True, right),
    }
    direct = {n: relayed[n] for n in (0, 1, 2, 5, 6)}
    direct[3] = (0, 2, False, whole)
    direct[7] = (2, 0, True, whole)
    kinds = [direct if straight[t] else relayed for t in range(3)]

    def going(t, n):
        back, step, other, lanes = kinds[t][n]
        return group_copy(t, n, owner(-back, False), owner(step, other), lanes, back == 0)

    def coming(t, n):
        back, step, other, lanes = kinds[t][n]
        return group_copy(t, n, owner(-back - step, other), owner(step, other), lanes, False)

    def own_copy(t):
        return pltpu.make_async_copy(
            mine.at[tiles[t]], full.at[ch, tiles[t]], store_sem.at[t]
        )

    def begin(t):
        for n in (0, 1, 3, 2) if straight[t] else (0, 1, 2):
            going(t, n).start()
        own_copy(t).start()

    def relay(t):
        coming(t, 0).wait_recv()
        if not straight[t]:
            going(t, 3).start()
        going(t, 5).start()
        coming(t, 1).wait_recv()
        if not straight[t]:
            going(t, 4).start()
        going(t, 6).start()

    def relay_far(t):
        coming(t, 3).wait_recv()
        going(t, 7).start()
        if not straight[t]:
            coming(t, 4).wait_recv()
            going(t, 8).start()

    def small_copy(i):
        return pltpu.make_async_remote_copy(
            src_ref=tight,
            dst_ref=shared.at[(seq % 2) * WAYS + ch],
            send_sem=s_send.at[i],
            recv_sem=s_recv,
            device_id={"seq": i, "ch": home},
            device_id_type=MESH,
        )

    def small_self(i):
        return jnp.logical_and(i == seq, at_home)

    def start_small(i, _):
        @pl.when(small_self(i))
        def _():
            pltpu.make_async_copy(tight, shared.at[(seq % 2) * WAYS + ch], s_recv).start()

        @pl.when(jnp.logical_not(small_self(i)))
        def _():
            small_copy(i).start()

        return 0

    groups = [range(0, 6), range(6, 11), range(11, count)]
    edges = [(0, 16), (16, 32), (32, TRIO)]
    for t in range(3):
        mix_channels(
            groups[t], rows, gains, bands, tables, projf, projr, gradf, small, skips, outs
        )
        pack(outs, mine, *edges[t])
        begin(t)
    finish_small(count, small, skips, tight)
    relay(0)
    lax.fori_loop(0, SHARDS, start_small, 0)
    relay(1)
    relay_far(0)
    relay(2)
    relay_far(1)
    relay_far(2)

    for v in range(2):
        for name, _ in names:
            feature_copy(v, name, False).wait_send()
    await_batch(0, r_send)
    await_batch(1, r_send)

    def end_sends(i, _):
        @pl.when(jnp.logical_not(is_self(i)))
        def _():
            grad_copy(2 * ch + i // WAYS, i % WAYS).wait_send()

        @pl.when(jnp.logical_not(small_self(i)))
        def _():
            small_copy(i).wait_send()

        return 0

    lax.fori_loop(0, SHARDS, end_sends, 0)

    @pl.when(at_home)
    def _():
        for i in range(1, WAYS):
            param_copy(i).wait_send()
            gain_copy(i).wait_send()

    for t in range(3):
        own_copy(t).wait()
        for n in kinds[t]:
            going(t, n).wait_send()
            if n in (2, 5, 6, 7, 8):
                coming(t, n).wait_recv()
    pltpu.make_async_copy(shared, shared, s_recv).wait()


def finish(
    count, features, full, shared, packed, wgrad, residue_out, rate_out, skip_out, rows
):
    block = count * WAYS
    tokens = full.shape[2]
    width = wgrad.shape[2]
    lanes = pl.ds(pl.multiple_of(pl.program_id(0) * width, width), width)
    right_side = features[:, :, lanes].reshape(tokens, width)
    product = mul(full[...].reshape(WAYS * TRIO, tokens), right_side)
    for part in range(rows.shape[0]):
        lanes = pl.ds(part * CHUNK, CHUNK)
        rows[part] = product[:, part * CHUNK : (part + 1) * CHUNK]
        for owner in range(WAYS):
            for g in range(3):
                own = rows[part, pl.ds(owner * TRIO + g, count, stride=3), :]
                wgrad[g, owner * count : (owner + 1) * count, lanes] = own

    @pl.when(pl.program_id(0) == 0)
    def _():
        half = ROWS // 2
        tiles = shared[...].reshape(2 * WAYS * half, CHUNK)
        turned = []
        for first in (0, half):
            pick = chosen(
                (2 * WAYS * half, 2 * block),
                lambda r, c: (r // half == c // count) & (r % half + first == c % count),
                F32,
            )
            turned.append(exact(tiles, pick, TN))
        turned = turned[0][: CHUNK // 2] + turned[1][CHUNK // 2 :]
        moment = turned[STATE : 2 * STATE] + turned[2 * STATE : 3 * STATE]
        residue_out[...] = turned[0:STATE]
        rate_out[...] = -packed[STATE:] * jnp.exp(packed[0:STATE]) * moment
        skip_out[...] = turned[3 * STATE : 3 * STATE + 1]


def local(features, qkv_weight, grad_out, residues, log_rates, skip_gain):
    width = features.shape[1]
    block = qkv_weight.shape[0]
    count = block // WAYS
    held, order = residues.shape
    weight = qkv_weight.transpose(1, 0, 2)
    anywhere = pl.BlockSpec(memory_space=pl.ANY)
    vmem = pl.BlockSpec(memory_space=pltpu.VMEM)
    dma = pltpu.SemaphoreType.DMA
    tokens = SHARDS * CHUNK
    operands = [
        pltpu.with_memory_space_constraint(array, pltpu.MemorySpace.HBM)
        for array in (
            features, weight, grad_out, log_rates.T, residues.T, skip_gain.reshape(1, held)
        )
    ]
    every, full, shared, packed = pl.pallas_call(
        functools.partial(kernel, count),
        out_shape=(
            jax.ShapeDtypeStruct((SHARDS, CHUNK, width), BF16),
            jax.ShapeDtypeStruct((WAYS, TRIO, tokens), BF16),
            jax.ShapeDtypeStruct((2 * WAYS, ROWS // 2, CHUNK), F32),
            jax.ShapeDtypeStruct((PARAM_ROWS, held), F32),
        ),
        in_specs=[anywhere] * 6,
        out_specs=(vmem,) * 4,
        scratch_shapes=[
            pltpu.VMEM((3, block, width), BF16),
            pltpu.VMEM((WAYS * TRIO, width), BF16),
            pltpu.VMEM((held, CHUNK), BF16),
            pltpu.VMEM((2 * WAYS, ROWS, CHUNK), BF16),
            pltpu.VMEM((SHARDS, WAYS, TRIO, CHUNK), BF16),
            pltpu.VMEM((WAYS, SHARDS, TRIO, CHUNK), BF16),
            pltpu.VMEM((SHARDS, ROWS, CHUNK), BF16),
            pltpu.VMEM((PARAM_ROWS, held), F32),
            pltpu.VMEM((2 * STATE, CHUNK), F32),
            pltpu.VMEM((ROWS, CHUNK), F32),
            pltpu.VMEM((ROWS, CHUNK), F32),
            pltpu.VMEM((ROWS, CHUNK, CHUNK), BF16),
            pltpu.VMEM((ROWS, 11 * STATE, CHUNK), BF16),
            pltpu.VMEM((SHARDS, TRIO, CHUNK), F32),
            pltpu.VMEM((SHARDS, TRIO, CHUNK), F32),
            pltpu.VMEM((SHARDS, ROWS, CHUNK), F32),
            pltpu.VMEM((SHARDS, TRIO, CHUNK), F32),
            pltpu.VMEM((ROWS, CHUNK), F32),
            pltpu.VMEM((ROWS, CHUNK), F32),
            pltpu.VMEM((1, held), F32),
            pltpu.VMEM((1, held), F32),
            pltpu.VMEM((TRIO, tokens), BF16),
            pltpu.VMEM((ROWS // 2, CHUNK), F32),
            dma((6,)),
            dma((2, 22)),
            dma((2, 22)),
            dma((2, WAYS)),
            dma((2, WAYS)),
            dma((SHARDS,)),
            dma,
            dma((WAYS,)),
            dma,
            dma((3, 9)),
            dma((3, 9)),
            dma((SHARDS,)),
            dma,
            pltpu.SemaphoreType.REGULAR((4,)),
            dma((WAYS,)),
            dma,
            dma((3,)),
        ],
        compiler_params=pltpu.CompilerParams(
            collective_id=0, has_side_effects=True, vmem_limit_bytes=24 * 2**20
        ),
    )(*operands)
    columns = 512

    def same(*shape):
        return pl.BlockSpec(shape, lambda n: (0,) * len(shape))

    weight_grad, residue_grad, rate_grad, skip_grad = pl.pallas_call(
        functools.partial(finish, count),
        grid=(width // columns,),
        out_shape=(
            jax.ShapeDtypeStruct((3, block, width), F32),
            jax.ShapeDtypeStruct((order, held), F32),
            jax.ShapeDtypeStruct((order, held), F32),
            jax.ShapeDtypeStruct((1, held), F32),
        ),
        in_specs=[
            vmem,
            vmem,
            vmem,
            vmem,
        ],
        out_specs=(
            pl.BlockSpec((3, block, columns), lambda n: (0, 0, n)),
            same(order, held),
            same(order, held),
            same(1, held),
        ),
        scratch_shapes=[pltpu.VMEM((columns // CHUNK, WAYS * TRIO, CHUNK), F32)],
        compiler_params=pltpu.CompilerParams(vmem_limit_bytes=24 * 2**20),
    )(every, full, shared, packed)
    return weight_grad.transpose(1, 0, 2), residue_grad.T, rate_grad.T, skip_grad.reshape(held)


def solution(mesh):
    placed = (
        P("seq", "ch"),
        P("seq", None, "ch"),
        P("ch", "seq"),
        P("ch", None),
        P("ch", None),
        P("ch"),
    )
    return jax.shard_map(
        local,
        mesh=mesh,
        in_specs=placed,
        out_specs=(P("seq", None, "ch"), P("ch", None), P("ch", None), P("ch")),
        check_vma=False,
    )
```
